32 devices in a mesh: chan: 4 (over x, core), seq: 8 (over z, y).
Axes of the slice: x: 2, y: 2, z: 4, core: 2. Of those that a mesh axis runs over, the one named last changes fastest.
Arguments:
- query: bfloat16 [4096, 512], P('seq', 'chan'), may hold values from -6 to 6
- key: bfloat16 [4096, 512], P('seq', 'chan'), may hold values from -6 to 6
- value: bfloat16 [4096, 512], P('seq', 'chan'), may hold values from -6 to 6
- filter_weights: bfloat16 [512, 8, 512], P('chan', 'seq'), may hold values from -6 to 6
- skip_gain: float32 [512], P('chan'), may hold values from 0.5 to 1.5
- cotangent: bfloat16 [4096, 512], P('seq', 'chan'), may hold values from -6 to 6
Outputs:
- mixed: bfloat16 [4096, 512], P('seq', 'chan')
- query_grad: bfloat16 [4096, 512], P('seq', 'chan')
- key_grad: bfloat16 [4096, 512], P('seq', 'chan')
- value_grad: bfloat16 [4096, 512], P('seq', 'chan')
- filter_grad: float32 [512, 8, 512], P('chan', 'seq')
The draws below stay inside these ranges and needn't reach their ends.
All inputs are finite; a program needn't handle non-finite values.
Results may differ from the reference program's by a relative error of at most 0.0085.
Values may be sent and summed in bfloat16 or wider, within the bound.
A program may use at most 64 MiB of HBM per device.

```python
import math
import jax
import jax.numpy as jnp
from jax import lax

TOK_DEV = 512
CH_DEV = 128
TOKENS = 4096
CHANNELS = 512
N_CHAN = 4
N_SEQ = 8


def levels(key, dims, split, low, top_value):
    level, own = 1.0, jax.random.fold_in(key, 6)
    for position, parts in split:
        draws = jnp.exp(jax.random.uniform(jax.random.fold_in(own, position), (parts,), jnp.float32, low / len(split), top_value / len(split)))
        level = level * jnp.repeat(draws, dims[position] // parts).reshape([-1 if axis == position else 1 for axis in range(len(dims))])
    return level


def gaussian(own_key, dims, spread, reach, pieces=(), held_as=jnp.bfloat16):
    entries = spread * jax.random.normal(own_key, dims, jnp.float32)
    if pieces:
        entries = entries * levels(own_key, dims, pieces, -0.22, 0.18)
    return jnp.clip(entries, -reach, reach).astype(held_as)


def setup_inputs(seed: int = 0) -> dict:
    key_list = jax.random.split(jax.random.key(seed), 7)
    return {
        "query": gaussian(key_list[0], (TOKENS, CHANNELS), 1.0, 6.0, ((0, 8), (1, 4))),
        "key": gaussian(key_list[1], (TOKENS, CHANNELS), 1.0, 6.0, ((0, 8), (1, 4))),
        "value": gaussian(key_list[2], (TOKENS, CHANNELS), 1.0, 6.0, ((0, 8), (1, 4))),
        "filter_weights": gaussian(key_list[3], (TOK_DEV, N_SEQ, CHANNELS), 1.0, 6.0, ((0, 4), (1, 8))),
        "skip_gain": jnp.clip(0.5 + 1.0 * jax.random.uniform(key_list[4], (CHANNELS,), jnp.float32) ** levels(key_list[4], (CHANNELS,), ((0, 4),), -0.2, 0.2), 0.5, 1.5),
        "cotangent": gaussian(key_list[5], (TOKENS, CHANNELS), 1.0, 6.0, ((0, 8), (1, 4))),
    }


def reference(query, key, value, filter_weights, skip_gain, cotangent):
    length = query.shape[0]
    width = query.shape[1]
    padded = 2 * length
    factor = 1.0 / math.sqrt(length)
    taps_all = filter_weights.astype(jnp.float32).transpose(1, 0, 2).reshape(length, width) * factor

    def split_groups(array_in):
        return array_in.reshape(length, N_CHAN, CH_DEV).transpose(1, 0, 2)

    def merge_groups(array_in):
        return array_in.transpose(1, 0, 2).reshape(length, N_CHAN * CH_DEV)

    def item_group(group_items):
        query_grp, key_grp, value_grp, grad_grp, gain_grp, taps_grp = group_items
        query_data = query_grp.astype(jnp.float32)
        key_data = key_grp.astype(jnp.float32)
        value_data = value_grp.astype(jnp.float32)
        grad_data = grad_grp.astype(jnp.float32)
        filter_spec = jnp.fft.rfft(taps_grp, n=padded, axis=0)
        mixed_in = key_data * value_data
        spec_in = jnp.fft.rfft(mixed_in, n=padded, axis=0)
        conv_out = jnp.fft.irfft(filter_spec * spec_in, n=padded, axis=0)[:length]
        state = conv_out + gain_grp[None, :] * mixed_in
        gate_grad = grad_data * query_data
        spec_grad = jnp.fft.rfft(gate_grad, n=padded, axis=0)
        back_grad = jnp.fft.irfft(jnp.conj(filter_spec) * spec_grad, n=padded, axis=0)[:length]
        back_grad = back_grad + gain_grp[None, :] * gate_grad
        filter_part = jnp.fft.irfft(jnp.conj(spec_in) * spec_grad, n=padded, axis=0)[:length]
        return ((query_data * state).astype(jnp.bfloat16), (grad_data * state).astype(jnp.bfloat16), (back_grad * value_data).astype(jnp.bfloat16), (back_grad * key_data).astype(jnp.bfloat16), filter_part * factor)
    gains = skip_gain.reshape(N_CHAN, CH_DEV)
    results = lax.map(item_group, (split_groups(query), split_groups(key), split_groups(value), split_groups(cotangent), gains, split_groups(taps_all)))
    filter_grad = merge_groups(results[4]).reshape(N_SEQ, length // N_SEQ, width).transpose(1, 0, 2)
    return (merge_groups(results[0]), merge_groups(results[1]), merge_groups(results[2]), merge_groups(results[3]), filter_grad)
```

```python
import functools
import math

import jax
import jax.numpy as jnp
import numpy as np
from jax import lax
from jax.experimental import pallas as pl
from jax.experimental.pallas import tpu as pltpu
from jax.sharding import PartitionSpec as P

MESH = pl.DeviceIdType.MESH
F32 = jnp.float32
BF16 = jnp.bfloat16
X, G, F = 0, 1, 2
GRAD, Y, BACK = 0, 1, 2


def split_table(table):
    high = jnp.asarray(table, F32).astype(BF16)
    low = (jnp.asarray(table, F32) - high.astype(F32)).astype(BF16)
    return high, low


def dot(a, b):
    return jnp.dot(a, b, preferred_element_type=F32)


def tables(slow, fast, factor):
    length = 2 * slow * fast
    kept = slow + 1
    padded = -(-kept // 8) * 8
    k1 = np.arange(kept)
    n1 = np.arange(slow)
    n2 = np.arange(fast)
    angle1 = 2.0 * np.pi * (np.outer(k1, n1) % (2 * slow)) / (2 * slow)
    first = np.zeros((2 * padded, slow))
    first[:kept] = np.cos(angle1)
    first[padded : padded + kept] = -np.sin(angle1)
    angle2 = 2.0 * np.pi * (np.outer(k1, n2) % length) / length
    twiddle = np.zeros((2, padded, fast))
    twiddle[0, :kept] = np.cos(angle2)
    twiddle[1, :kept] = -np.sin(angle2)
    angle3 = 2.0 * np.pi * (np.outer(n2, n2) % fast) / fast
    cosine, sine = np.cos(angle3), np.sin(angle3)
    ahead = np.block([[cosine, -sine], [sine, cosine]])
    back = np.block([[cosine, sine], [-sine, cosine]])
    weight = np.where((k1 == 0) | (k1 == slow), 1.0, 2.0)[:, None] * (factor / length)
    last = np.zeros((slow, 2 * padded))
    last[:, :kept] = (weight * np.cos(angle1)).T
    last[:, padded : padded + kept] = (-weight * np.sin(angle1)).T
    return padded, first, twiddle, ahead, back, last


def core_kernel(
    n_chan, n_seq, padded, n_const, *refs
):
    q_hbm, k_hbm, v_hbm, g_hbm, w_hbm, gain_ref = refs[:6]
    const_hbm = refs[6 : 6 + n_const]
    out_sig, out_tap, out_gain = refs[6 + n_const : 9 + n_const]
    (
        q_ref, k_ref, v_ref, g_ref, in_tap, send_sig, in_sig, res_sig, lines, turned, spec,
    ) = refs[9 + n_const : 20 + n_const]
    consts = refs[20 + n_const : 20 + 2 * n_const]
    (
        load_sem, const_sem, own_sem, s_send, s_recv, t_send, t_recv, r_send, r_recv, b_send, b_recv,
    ) = refs[20 + 2 * n_const :]
    first_ref, twid_ref, ahead_h, ahead_l, back_h, back_l, last_ref = consts
    chan, seq = lax.axis_index("chan"), lax.axis_index("seq")
    _, _, pieces, group, fast = send_sig.shape
    slow = n_seq * pieces
    width = n_seq * group

    def each(count, act):
        def step(d, carry):
            act(d)
            return carry

        lax.fori_loop(1, count, step, 0)

    barrier = pltpu.get_barrier_semaphore()

    def greet(device):
        pl.semaphore_signal(barrier, inc=1, device_id=device, device_id_type=MESH)

    def seq_to(d):
        return lax.rem(seq + d, n_seq)

    def seq_from(d):
        return lax.rem(seq + n_seq - d, n_seq)

    def chan_to(d):
        return lax.rem(chan + d, n_chan)

    def chan_from(d):
        return lax.rem(chan + n_chan - d, n_chan)

    each(n_seq, lambda d: greet((chan, seq_to(d))))
    each(n_chan, lambda d: greet((chan_to(d), seq)))

    loads = [
        pltpu.make_async_copy(source, target, load_sem.at[i])
        for i, (source, target) in enumerate(
            [(k_hbm, k_ref), (v_hbm, v_ref), (g_hbm, g_ref), (q_hbm, q_ref)]
        )
    ]
    for copy in loads:
        copy.start()
    const_loads = [
        pltpu.make_async_copy(source, target, const_sem.at[i])
        for i, (source, target) in enumerate(zip(const_hbm, consts))
    ]
    for copy in const_loads:
        copy.start()
    out_gain[...] = gain_ref[...]

    def remote(source, target, send, recv, device):
        return pltpu.make_async_remote_copy(
            src_ref=source, dst_ref=target, send_sem=send, recv_sem=recv,
            device_id=device, device_id_type=MESH,
        )

    def sig_copy(slot, d, landing):
        there = seq_to(d)
        return remote(
            send_sig.at[slot, there], in_sig.at[slot, landing],
            s_send.at[slot, d], s_recv.at[slot, d], (chan, there),
        )

    def res_copy(slot, d, landing):
        there = seq_to(d)
        return remote(
            res_sig.at[slot, there], out_sig.at[slot, landing],
            r_send.at[slot, d], r_recv.at[slot, d], (chan, there),
        )

    def taps_of(at):
        return w_hbm.at[:, pl.ds(pl.multiple_of(at * width, width), width)]

    def tap_copy(d, landing):
        there = chan_to(d)
        return remote(
            taps_of(there), in_tap.at[landing], t_send.at[d], t_recv.at[d], (there, seq)
        )

    def back_copy(d, landing):
        there = chan_to(d)
        return remote(
            out_sig.at[GRAD, :, there], out_tap.at[landing], b_send.at[d], b_recv.at[d], (there, seq)
        )

    def own_copy(source, target, index):
        return pltpu.make_async_copy(source, target, own_sem.at[index])

    own_sig = [own_copy(send_sig.at[i, seq], in_sig.at[i, seq], i) for i in range(3)]
    own_res = [own_copy(res_sig.at[i, seq], out_sig.at[i, seq], 3 + i) for i in range(3)]
    own_taps = own_copy(taps_of(chan), in_tap.at[chan], 6)
    own_back = own_copy(out_sig.at[GRAD, :, chan], out_tap.at[chan], 7)
    own_taps.start()

    def pack(slot, pick):
        for u in range(pieces):
            flipped = pick(u).T
            for t in range(n_seq):
                send_sig[slot, t, u] = flipped[t * group : (t + 1) * group].astype(BF16)

    def product(a_ref, b_ref):
        def pick(u):
            rows = pl.ds(u * fast, fast)
            return a_ref[rows, :].astype(F32) * b_ref[rows, :].astype(F32)

        return pick

    def send(slot):
        each(n_seq, lambda d: sig_copy(slot, d, seq).start())
        own_sig[slot].start()

    loads[0].wait()
    loads[1].wait()
    pack(X, product(k_ref, v_ref))
    pl.semaphore_wait(barrier, n_chan + n_seq - 2)
    each(n_chan, lambda d: tap_copy(d, chan).start())
    send(X)
    loads[2].wait()
    loads[3].wait()
    pack(G, product(g_ref, q_ref))
    send(G)
    own_taps.wait()
    each(n_chan, lambda d: tap_copy(d, chan_from(d)).wait())
    pack(F, lambda u: in_tap[u].astype(F32))
    send(F)
    for copy in const_loads:
        copy.wait()

    cosine, sine = twid_ref[0], twid_ref[1]
    joint = fast % 128 == 0 and group % 2 == 0
    batch = 2 if joint else 1

    def times(table, columns):
        if not joint:
            return [dot(table, column) for column in columns]
        wide = dot(table, jnp.concatenate(columns, axis=1))
        return [wide[:, i * fast : (i + 1) * fast] for i in range(len(columns))]

    def through(x, high, low):
        short = x.astype(BF16)
        return dot(short, high[...]) + dot(short, low[...])

    def forward(slot):
        own_sig[slot].wait()
        each(n_seq, lambda d: sig_copy(slot, d, seq_from(d)).wait())
        for s in range(n_seq):
            for u in range(pieces):
                at = pl.ds((s * pieces + u) * group, group)
                lines[slot, at, :] = in_sig[slot, s, u].astype(F32)
        for base in range(0, group, batch):
            columns = []
            for c in range(base, base + batch):
                column = lines[slot, pl.ds(c, slow, stride=group), :].astype(BF16)
                columns.append(jnp.concatenate([column, column], axis=0))
            for c, got in zip(range(base, base + batch), times(first_ref[...], columns)):
                real, imag = got[:padded], got[padded:]
                at = pl.ds(c * padded, padded)
                turned[slot, at, :fast] = real * cosine - imag * sine
                turned[slot, at, fast:] = real * sine + imag * cosine
        turned[slot] = through(turned[slot], ahead_h, ahead_l)

    def inverse(slot, a, b, conjugate):
        for c in range(group):
            at = pl.ds(c * padded, padded)
            ar, ai = turned[a, at, :fast], turned[a, at, fast:]
            br, bi = turned[b, at, :fast], turned[b, at, fast:]
            if conjugate:
                spec[slot, at, :fast] = ar * br + ai * bi
                spec[slot, at, fast:] = ar * bi - ai * br
            else:
                spec[slot, at, :fast] = ar * br - ai * bi
                spec[slot, at, fast:] = ar * bi + ai * br
        spec[slot] = through(spec[slot], back_h, back_l)
        for base in range(0, group, batch):
            columns = []
            for c in range(base, base + batch):
                at = pl.ds(c * padded, padded)
                real, imag = spec[slot, at, :fast], spec[slot, at, fast:]
                real, imag = real * cosine + imag * sine, imag * cosine - real * sine
                both = jnp.concatenate([real, imag], axis=0).astype(BF16)
                columns.append(jnp.concatenate([both, both], axis=0))
            for c, got in zip(range(base, base + batch), times(last_ref[...], columns)):
                lines[slot, pl.ds(c, slow, stride=group), :] = got
        for s in range(n_seq):
            for u in range(pieces):
                at = pl.ds((s * pieces + u) * group, group)
                res_sig[slot, s, u] = lines[slot, at, :].astype(BF16)
        each(n_seq, lambda d: res_copy(slot, d, seq).start())
        own_res[slot].start()

    forward(X)
    forward(G)
    inverse(GRAD, X, G, True)
    forward(F)
    inverse(Y, F, X, False)
    inverse(BACK, F, G, True)

    def arrive(slot):
        own_res[slot].wait()
        each(n_seq, lambda d: res_copy(slot, d, seq_from(d)).wait())

    arrive(GRAD)
    each(n_chan, lambda d: back_copy(d, chan).start())
    own_back.start()
    arrive(Y)
    arrive(BACK)
    own_back.wait()
    each(n_chan, lambda d: back_copy(d, chan_from(d)).wait())


def after_kernel(
    q_ref, k_ref, v_ref, g_ref, gain_ref, sig_ref, tap_ref, m_ref, qg_ref, kg_ref, vg_ref, fg_ref, hold
):
    _, seq_parts, pieces, group, fast = sig_ref.shape
    gain = gain_ref[...]

    def columns(pick):
        for t in range(seq_parts):
            hold[pl.ds(t * group, group), :] = pick(t).astype(F32)
        return hold[...].T

    for u in range(pieces):
        rows = pl.ds(u * fast, fast)
        query, key = q_ref[rows, :].astype(F32), k_ref[rows, :].astype(F32)
        value, grad = v_ref[rows, :].astype(F32), g_ref[rows, :].astype(F32)
        state = columns(lambda t: sig_ref[Y, t, u]) + gain * (key * value)
        m_ref[rows, :] = (query * state).astype(BF16)
        qg_ref[rows, :] = (grad * state).astype(BF16)
        back = columns(lambda t: sig_ref[BACK, t, u]) + gain * (grad * query)
        kg_ref[rows, :] = (back * value).astype(BF16)
        vg_ref[rows, :] = (back * key).astype(BF16)
    for a in range(pieces):
        got = columns(lambda t: tap_ref[a, t])
        fg_ref[pl.ds(a, fast, stride=pieces), :] = got


def body(n_chan, n_seq, query, key, value, filter_weights, skip_gain, cotangent):
    rows, width = query.shape
    tap_rows, _, all_width = filter_weights.shape
    fast, group, pieces = tap_rows, width // n_seq, n_chan
    slow = rows * n_seq // fast
    padded, first, twiddle, ahead, back, last = tables(slow, fast, 1.0 / math.sqrt(rows * n_seq))
    weights = filter_weights.reshape(tap_rows, all_width)
    consts = [
        jnp.concatenate(split_table(first), axis=1),
        jnp.asarray(twiddle, F32),
        *split_table(ahead),
        *split_table(back),
        jnp.concatenate(split_table(last), axis=1),
    ]
    sig_dims = (3, n_seq, pieces, group, fast)
    tap_dims = (n_chan, n_seq, group, fast)
    flat_dims = (rows, width)
    dma = pltpu.SemaphoreType.DMA
    anywhere = pl.BlockSpec(memory_space=pl.ANY)
    vmem = pl.BlockSpec(memory_space=pltpu.VMEM)
    sig, taps, gain = pl.pallas_call(
        functools.partial(core_kernel, n_chan, n_seq, padded, len(consts)),
        out_shape=[pltpu.VMEM(sig_dims, BF16), pltpu.VMEM(tap_dims, BF16), pltpu.VMEM((1, width), F32)],
        in_specs=[anywhere] * 5 + [vmem] + [anywhere] * len(consts),
        out_specs=[vmem] * 3,
        scratch_shapes=[
            *[pltpu.VMEM(flat_dims, BF16)] * 4,
            pltpu.VMEM((n_chan, tap_rows, width), BF16),
            *[pltpu.VMEM(sig_dims, BF16)] * 3,
            pltpu.VMEM((3, slow * group, fast), F32),
            pltpu.VMEM((3, group * padded, 2 * fast), F32),
            pltpu.VMEM((3, group * padded, 2 * fast), F32),
            *[pltpu.VMEM(const.shape, const.dtype) for const in consts],
            dma((4,)),
            dma((len(consts),)),
            dma((8,)),
            dma((3, n_seq)),
            dma((3, n_seq)),
            dma((n_chan,)),
            dma((n_chan,)),
            dma((3, n_seq)),
            dma((3, n_seq)),
            dma((n_chan,)),
            dma((n_chan,)),
        ],
        compiler_params=pltpu.CompilerParams(
            collective_id=0, has_side_effects=True, vmem_limit_bytes=60 * 1024 * 1024
        ),
        name="core",
    )(query, key, value, cotangent, weights, skip_gain.reshape(1, width), *consts)
    flat = jax.ShapeDtypeStruct(flat_dims, BF16)
    outs = pl.pallas_call(
        after_kernel,
        out_shape=[flat, flat, flat, flat, jax.ShapeDtypeStruct((tap_rows * n_chan, width), F32)],
        in_specs=[vmem] * 7,
        out_specs=[vmem] * 5,
        scratch_shapes=[pltpu.VMEM((width, fast), F32)],
        compiler_params=pltpu.CompilerParams(vmem_limit_bytes=24 * 1024 * 1024),
        name="after",
    )(query, key, value, cotangent, gain, sig, taps)
    return (*outs[:4], outs[4].reshape(tap_rows, 1, all_width))


def solution(mesh):
    n_chan, n_seq = mesh.shape["chan"], mesh.shape["seq"]
    block = P("seq", "chan")
    taps = P("chan", "seq", None)
    return jax.shard_map(
        functools.partial(body, n_chan, n_seq),
        mesh=mesh,
        in_specs=(block, block, block, taps, P("chan"), block),
        out_specs=(block, block, block, block, taps),
        check_vma=False,
    )
```

```python
import functools
import math

import jax
import jax.numpy as jnp
import numpy as np
from jax import lax
from jax.experimental import pallas as pl
from jax.experimental.pallas import tpu as pltpu
from jax.sharding import PartitionSpec as P

MESH = pl.DeviceIdType.MESH
F32 = jnp.float32
BF16 = jnp.bfloat16
X, G, F = 0, 1, 2
Y, BACK, GRAD = 0, 1, 2
PAIR, LONE = 0, 1


def split_table(table):
    high = jnp.asarray(table, F32).astype(BF16)
    low = (jnp.asarray(table, F32) - high.astype(F32)).astype(BF16)
    return high, low


def dot(a, b):
    return jnp.dot(a, b, preferred_element_type=F32)


def tables(slow, fast, factor):
    length = 2 * slow * fast
    kept = slow + 1
    padded = -(-kept // 8) * 8
    k1 = np.arange(kept)
    n1 = np.arange(slow)
    n2 = np.arange(fast)
    angle1 = 2.0 * np.pi * (np.outer(k1, n1) % (2 * slow)) / (2 * slow)
    first = np.zeros((2 * padded, slow))
    first[:kept] = np.cos(angle1)
    first[padded : padded + kept] = -np.sin(angle1)
    angle2 = 2.0 * np.pi * (np.outer(k1, n2) % length) / length
    twiddle = np.zeros((2, padded, fast))
    twiddle[0, :kept] = np.cos(angle2)
    twiddle[1, :kept] = -np.sin(angle2)
    angle3 = 2.0 * np.pi * (np.outer(n2, n2) % fast) / fast
    cosine, sine = np.cos(angle3), np.sin(angle3)
    ahead = np.block([[cosine, -sine], [sine, cosine]])
    back = np.block([[cosine, sine], [-sine, cosine]])
    weight = np.where((k1 == 0) | (k1 == slow), 1.0, 2.0)[:, None] * (factor / length)
    last = np.zeros((slow, 2 * padded))
    last[:, :kept] = (weight * np.cos(angle1)).T
    last[:, padded : padded + kept] = (-weight * np.sin(angle1)).T
    return padded, first, twiddle, ahead, back, last


def core_kernel(
    n_chan, n_seq, padded, n_const, *refs
):
    q_hbm, k_hbm, v_hbm, g_hbm, w_hbm, gain_hbm = refs[:6]
    const_hbm = refs[6 : 6 + n_const]
    out_pair, out_tap, out_gain = refs[6 + n_const : 9 + n_const]
    (
        q_ref, k_ref, v_ref, g_ref, in_tap, send_pair, in_pair, res_pair, send_lone, in_lone, res_lone, out_lone,
        lines, turned, spec,
    ) = refs[9 + n_const : 24 + n_const]
    consts = refs[24 + n_const : 24 + 2 * n_const]
    (
        load_sem, const_sem, own_sem, s_send, s_recv, t_send, t_recv, r_send, r_recv, b_send, b_recv,
    ) = refs[24 + 2 * n_const :]
    first_ref, twid_ref, ahead_h, ahead_l, back_h, back_l, last_ref = consts
    chan, seq = lax.axis_index("chan"), lax.axis_index("seq")
    _, pieces, group, fast = send_lone.shape
    slow = n_seq * pieces
    width = n_seq * group

    def each(count, act):
        def step(d, carry):
            act(d)
            return carry

        lax.fori_loop(1, count, step, 0)

    barrier = pltpu.get_barrier_semaphore()

    def greet(device):
        pl.semaphore_signal(barrier, inc=1, device_id=device, device_id_type=MESH)

    def span(low, high, act):
        def step(i, carry):
            act(i)
            return carry

        lax.fori_loop(low, high, step, 0)

    def others(act, own, count):
        each(count, lambda d: act(lax.rem(own + d, count)))

    loads = [
        pltpu.make_async_copy(source, target, load_sem.at[i])
        for i, (source, target) in enumerate(
            [(k_hbm, k_ref), (v_hbm, v_ref), (g_hbm, g_ref), (q_hbm, q_ref), (gain_hbm, out_gain)]
        )
    ]
    for copy in loads[:2]:
        copy.start()
    others(lambda i: greet((chan, i)), seq, n_seq)
    others(lambda i: greet((i, seq)), chan, n_chan)
    for copy in loads[2:]:
        copy.start()
    const_loads = [
        pltpu.make_async_copy(source, target, const_sem.at[i])
        for i, (source, target) in enumerate(zip(const_hbm, consts))
    ]

    def remote(source, target, send, recv, device):
        return pltpu.make_async_remote_copy(
            src_ref=source, dst_ref=target, send_sem=send, recv_sem=recv,
            device_id=device, device_id_type=MESH,
        )

    def at_slot(pair, lone, slot, peer, u):
        return lone.at[peer, u] if slot == 2 else pair.at[peer, slot, u]

    def sig_copy(kind, there, landing):
        source, target = ((send_pair, in_pair), (send_lone, in_lone))[kind]
        return remote(
            source.at[there], target.at[landing],
            s_send.at[kind, there], s_recv.at[kind, landing], (chan, there),
        )

    def res_copy(kind, there, landing):
        source, target = ((res_pair, out_pair), (res_lone, out_lone))[kind]
        return remote(
            source.at[there], target.at[landing],
            r_send.at[kind, there], r_recv.at[kind, landing], (chan, there),
        )

    def taps_of(at):
        return w_hbm.at[:, pl.ds(pl.multiple_of(at * width, width), width)]

    def tap_copy(there, landing):
        return remote(
            taps_of(there), in_tap.at[landing], t_send.at[there], t_recv.at[landing], (there, seq)
        )

    def back_copy(there, landing):
        return remote(
            out_lone.at[:, there], out_tap.at[landing], b_send.at[there], b_recv.at[landing],
            (there, seq),
        )

    def own_copy(source, target, index):
        return pltpu.make_async_copy(source, target, own_sem.at[index])

    own_sig = [
        own_copy(send_pair.at[seq], in_pair.at[seq], 0), own_copy(send_lone.at[seq], in_lone.at[seq], 1)
    ]
    own_res = [
        own_copy(res_pair.at[seq], out_pair.at[seq], 2), own_copy(res_lone.at[seq], out_lone.at[seq], 3)
    ]
    own_taps = own_copy(taps_of(chan), in_tap.at[chan], 4)
    own_back = own_copy(out_lone.at[:, chan], out_tap.at[chan], 5)
    own_taps.start()

    def pack(slot, pick):
        for u in range(pieces):
            flipped = pick(u).T
            for t in range(n_seq):
                at_slot(send_pair, send_lone, slot, t, u)[...] = flipped[t * group : (t + 1) * group].astype(BF16)

    def product(a_ref, b_ref):
        def pick(u):
            rows = pl.ds(u * fast, fast)
            return a_ref[rows, :].astype(F32) * b_ref[rows, :].astype(F32)

        return pick

    def send(kind):
        others(lambda i: sig_copy(kind, i, seq).start(), seq, n_seq)
        own_sig[kind].start()

    loads[0].wait()
    loads[1].wait()
    pack(X, product(k_ref, v_ref))
    loads[2].wait()
    loads[3].wait()
    pack(G, product(g_ref, q_ref))
    pl.semaphore_wait(barrier, n_seq + n_chan - 2)
    others(lambda i: tap_copy(i, chan).start(), chan, n_chan)
    send(PAIR)
    for copy in const_loads:
        copy.start()
    own_taps.wait()
    others(lambda i: tap_copy(i, i).wait(), chan, n_chan)
    pack(F, lambda u: in_tap[u].astype(F32))
    send(LONE)
    for copy in const_loads:
        copy.wait()

    cosine, sine = twid_ref[0], twid_ref[1]
    joint = fast % 128 == 0 and group % 2 == 0
    batch = 2 if joint else 1

    def times(table, columns):
        if not joint:
            return [dot(table, column) for column in columns]
        wide = dot(table, jnp.concatenate(columns, axis=1))
        return [wide[:, i * fast : (i + 1) * fast] for i in range(len(columns))]

    def through(x, high, low):
        short = x.astype(BF16)
        return dot(short, high[...]) + dot(short, low[...])

    def forward(slot):
        for s in range(n_seq):
            for u in range(pieces):
                at = pl.ds((s * pieces + u) * group, group)
                lines[slot, at, :] = at_slot(in_pair, in_lone, slot, s, u)[...].astype(F32)
        for base in range(0, group, batch):
            columns = []
            for c in range(base, base + batch):
                column = lines[slot, pl.ds(c, slow, stride=group), :].astype(BF16)
                columns.append(jnp.concatenate([column, column], axis=0))
            for c, got in zip(range(base, base + batch), times(first_ref[...], columns)):
                real, imag = got[:padded], got[padded:]
                at = pl.ds(c * padded, padded)
                turned[slot, at, :fast] = real * cosine - imag * sine
                turned[slot, at, fast:] = real * sine + imag * cosine
        turned[slot] = through(turned[slot], ahead_h, ahead_l)

    def inverse(slot, a, b, conjugate):
        for c in range(group):
            at = pl.ds(c * padded, padded)
            ar, ai = turned[a, at, :fast], turned[a, at, fast:]
            br, bi = turned[b, at, :fast], turned[b, at, fast:]
            if conjugate:
                spec[slot, at, :fast] = ar * br + ai * bi
                spec[slot, at, fast:] = ar * bi - ai * br
            else:
                spec[slot, at, :fast] = ar * br - ai * bi
                spec[slot, at, fast:] = ar * bi + ai * br
        spec[slot] = through(spec[slot], back_h, back_l)
        for base in range(0, group, batch):
            columns = []
            for c in range(base, base + batch):
                at = pl.ds(c * padded, padded)
                real, imag = spec[slot, at, :fast], spec[slot, at, fast:]
                real, imag = real * cosine + imag * sine, imag * cosine - real * sine
                both = jnp.concatenate([real, imag], axis=0).astype(BF16)
                columns.append(jnp.concatenate([both, both], axis=0))
            for c, got in zip(range(base, base + batch), times(last_ref[...], columns)):
                lines[slot, pl.ds(c, slow, stride=group), :] = got
        for s in range(n_seq):
            for u in range(pieces):
                at = pl.ds((s * pieces + u) * group, group)
                at_slot(res_pair, res_lone, slot, s, u)[...] = lines[slot, at, :].astype(BF16)

    def landed(kind):
        own_sig[kind].wait()
        others(lambda i: sig_copy(kind, i, i).wait(), seq, n_seq)

    def reply(kind):
        others(lambda i: res_copy(kind, i, seq).start(), seq, n_seq)
        own_res[kind].start()

    def arrive(kind):
        own_res[kind].wait()
        others(lambda i: res_copy(kind, i, i).wait(), seq, n_seq)

    landed(PAIR)
    forward(X)
    forward(G)
    inverse(GRAD, X, G, True)
    reply(LONE)
    landed(LONE)
    forward(F)
    inverse(Y, F, X, False)
    inverse(BACK, F, G, True)
    reply(PAIR)
    arrive(LONE)
    others(lambda i: back_copy(i, chan).start(), chan, n_chan)
    own_back.start()
    arrive(PAIR)
    own_back.wait()
    loads[4].wait()
    others(lambda i: back_copy(i, i).wait(), chan, n_chan)


def after_kernel(
    q_ref, k_ref, v_ref, g_ref, gain_ref, sig_ref, tap_ref, m_ref, qg_ref, kg_ref, vg_ref, fg_ref, hold
):
    seq_parts, _, pieces, group, fast = sig_ref.shape
    gain = gain_ref[...]

    def columns(pick):
        for t in range(seq_parts):
            hold[pl.ds(t * group, group), :] = pick(t).astype(F32)
        return hold[...].T

    for u in range(pieces):
        rows = pl.ds(u * fast, fast)
        query, key = q_ref[rows, :].astype(F32), k_ref[rows, :].astype(F32)
        value, grad = v_ref[rows, :].astype(F32), g_ref[rows, :].astype(F32)
        state = columns(lambda t: sig_ref[t, Y, u]) + gain * (key * value)
        m_ref[rows, :] = (query * state).astype(BF16)
        qg_ref[rows, :] = (grad * state).astype(BF16)
        back = columns(lambda t: sig_ref[t, BACK, u]) + gain * (grad * query)
        kg_ref[rows, :] = (back * value).astype(BF16)
        vg_ref[rows, :] = (back * key).astype(BF16)
    for a in range(pieces):
        got = columns(lambda t: tap_ref[a, t])
        fg_ref[pl.ds(a, fast, stride=pieces), :] = got


def body(n_chan, n_seq, query, key, value, filter_weights, skip_gain, cotangent):
    rows, width = query.shape
    tap_rows, _, all_width = filter_weights.shape
    fast, group, pieces = tap_rows, width // n_seq, n_chan
    slow = rows * n_seq // fast
    padded, first, twiddle, ahead, back, last = tables(slow, fast, 1.0 / math.sqrt(rows * n_seq))
    weights = filter_weights.reshape(tap_rows, all_width)
    consts = [
        jnp.concatenate(split_table(first), axis=1),
        jnp.asarray(twiddle, F32),
        *split_table(ahead),
        *split_table(back),
        jnp.concatenate(split_table(last), axis=1),
    ]
    pair_dims = (n_seq, 2, pieces, group, fast)
    lone_dims = (n_seq, pieces, group, fast)
    tap_dims = (n_chan, n_seq, group, fast)
    flat_dims = (rows, width)
    dma = pltpu.SemaphoreType.DMA
    anywhere = pl.BlockSpec(memory_space=pl.ANY)
    vmem = pl.BlockSpec(memory_space=pltpu.VMEM)
    sig, taps, gain = pl.pallas_call(
        functools.partial(core_kernel, n_chan, n_seq, padded, len(consts)),
        out_shape=[pltpu.VMEM(pair_dims, BF16), pltpu.VMEM(tap_dims, BF16), pltpu.VMEM((1, width), F32)],
        in_specs=[anywhere] * (6 + len(consts)),
        out_specs=[vmem] * 3,
        scratch_shapes=[
            *[pltpu.VMEM(flat_dims, BF16)] * 4,
            pltpu.VMEM((n_chan, tap_rows, width), BF16),
            *[pltpu.VMEM(pair_dims, BF16)] * 3,
            *[pltpu.VMEM(lone_dims, BF16)] * 4,
            pltpu.VMEM((3, slow * group, fast), F32),
            pltpu.VMEM((3, group * padded, 2 * fast), F32),
            pltpu.VMEM((3, group * padded, 2 * fast), F32),
            *[pltpu.VMEM(const.shape, const.dtype) for const in consts],
            dma((5,)),
            dma((len(consts),)),
            dma((6,)),
            dma((2, n_seq)),
            dma((2, n_seq)),
            dma((n_chan,)),
            dma((n_chan,)),
            dma((2, n_seq)),
            dma((2, n_seq)),
            dma((n_chan,)),
            dma((n_chan,)),
        ],
        compiler_params=pltpu.CompilerParams(
            collective_id=0, has_side_effects=True, vmem_limit_bytes=60 * 1024 * 1024
        ),
        name="core",
    )(query, key, value, cotangent, weights, skip_gain.reshape(1, width), *consts)
    flat = jax.ShapeDtypeStruct(flat_dims, BF16)
    outs = pl.pallas_call(
        after_kernel,
        out_shape=[flat, flat, flat, flat, jax.ShapeDtypeStruct((tap_rows * n_chan, width), F32)],
        in_specs=[vmem] * 7,
        out_specs=[vmem] * 5,
        scratch_shapes=[pltpu.VMEM((width, fast), F32)],
        compiler_params=pltpu.CompilerParams(vmem_limit_bytes=24 * 1024 * 1024),
        name="after",
    )(query, key, value, cotangent, gain, sig, taps)
    return (*outs[:4], outs[4].reshape(tap_rows, 1, all_width))


def solution(mesh):
    n_chan, n_seq = mesh.shape["chan"], mesh.shape["seq"]
    block = P("seq", "chan")
    taps = P("chan", "seq", None)
    return jax.shard_map(
        functools.partial(body, n_chan, n_seq),
        mesh=mesh,
        in_specs=(block, block, block, taps, P("chan"), block),
        out_specs=(block, block, block, block, taps),
        check_vma=False,
    )
```

```python
import functools
import math

import jax
import jax.numpy as jnp
import numpy as np
from jax import lax
from jax.experimental import pallas as pl
from jax.experimental.pallas import tpu as pltpu
from jax.sharding import PartitionSpec as P

MESH = pl.DeviceIdType.MESH
F32 = jnp.float32
BF16 = jnp.bfloat16
X, G, F = 0, 1, 2
Y, BACK, GRAD = 0, 1, 2
PAIR, LONE = 0, 1


def split_table(table):
    high = jnp.asarray(table, F32).astype(BF16)
    low = (jnp.asarray(table, F32) - high.astype(F32)).astype(BF16)
    return high, low


def dot(a, b):
    return jnp.dot(a, b, preferred_element_type=F32)


def tables(slow, fast, factor, tile):
    length = 2 * slow * fast
    kept = slow + 1
    padded = -(-kept // tile) * tile
    k1 = np.arange(kept)
    n1 = np.arange(slow)
    n2 = np.arange(fast)
    angle1 = 2.0 * np.pi * (np.outer(k1, n1) % (2 * slow)) / (2 * slow)
    first = np.zeros((2 * padded, slow))
    first[:kept] = np.cos(angle1)
    first[padded : padded + kept] = -np.sin(angle1)
    angle2 = 2.0 * np.pi * (np.outer(k1, n2) % length) / length
    twiddle = np.zeros((2, padded, fast))
    twiddle[0, :kept] = np.cos(angle2)
    twiddle[1, :kept] = -np.sin(angle2)
    angle3 = 2.0 * np.pi * (np.outer(n2, n2) % fast) / fast
    cosine, sine = np.cos(angle3), np.sin(angle3)
    ahead = np.block([[cosine, -sine], [sine, cosine]])
    back = np.block([[cosine, sine], [-sine, cosine]])
    weight = np.where((k1 == 0) | (k1 == slow), 1.0, 2.0)[:, None] * (factor / length)
    last = np.zeros((slow, 2 * padded))
    last[:, :kept] = (weight * np.cos(angle1)).T
    last[:, padded : padded + kept] = (-weight * np.sin(angle1)).T
    return padded, first, twiddle, ahead, back, last


def joined(fast, group):
    return 2 if fast % 128 == 0 and group % 2 == 0 else 1


def core_kernel(n_chan, n_seq, padded, n_const, *refs):
    q_hbm, k_hbm, v_hbm, g_hbm, w_hbm, gain_hbm = refs[:6]
    const_hbm = refs[6 : 6 + n_const]
    out_pair, out_tap, out_gain = refs[6 + n_const : 9 + n_const]
    (
        q_ref, k_ref, v_ref, g_ref, in_tap, send_pair, in_pair, res_pair, send_lone, in_lone, res_lone, out_lone,
        lines, short, turned, spec,
    ) = refs[9 + n_const : 25 + n_const]
    consts = refs[25 + n_const : 25 + 2 * n_const]
    (
        load_sem, const_sem, own_sem, s_send, s_recv, t_send, t_recv, r_send, r_recv, b_send, b_recv,
        seq_ready, chan_ready,
    ) = refs[25 + 2 * n_const :]
    first_ref, twid_ref, ahead_ref, back_ref, last_ref = consts
    chan, seq = lax.axis_index("chan"), lax.axis_index("seq")
    _, pieces, group, fast = send_lone.shape
    slow = n_seq * pieces
    width = n_seq * group

    def each(count, act):
        def step(d, carry):
            act(d)
            return carry

        lax.fori_loop(1, count, step, 0)

    barrier = pltpu.get_barrier_semaphore()

    def greet(device):
        pl.semaphore_signal(barrier, inc=1, device_id=device, device_id_type=MESH)

    def tell(ready, device):
        pl.semaphore_signal(ready, inc=1, device_id=device, device_id_type=MESH)

    def span(low, high, act):
        def step(i, carry):
            act(i)
            return carry

        lax.fori_loop(low, high, step, 0)

    def others(act, own, count):
        each(count, lambda d: act(lax.rem(own + d, count)))

    loads = [
        pltpu.make_async_copy(source, target, load_sem.at[i])
        for i, (source, target) in enumerate(
            [(k_hbm, k_ref), (v_hbm, v_ref), (g_hbm, g_ref), (q_hbm, q_ref), (gain_hbm, out_gain)]
        )
    ]
    for copy in loads[:2]:
        copy.start()
    others(lambda i: greet((chan, i)), seq, n_seq)
    span(chan + 1, n_chan, lambda i: greet((i, seq)))
    for copy in loads[2:]:
        copy.start()
    const_loads = [
        pltpu.make_async_copy(source, target, const_sem.at[i])
        for i, (source, target) in enumerate(zip(const_hbm, consts))
    ]

    def remote(source, target, send, recv, device):
        return pltpu.make_async_remote_copy(
            src_ref=source, dst_ref=target, send_sem=send, recv_sem=recv,
            device_id=device, device_id_type=MESH,
        )

    def at_slot(pair, lone, slot, peer, u):
        return lone.at[peer, u] if slot == 2 else pair.at[peer, slot, u]

    def sig_copy(kind, there, landing):
        source, target = ((send_pair, in_pair), (send_lone, in_lone))[kind]
        return remote(
            source.at[there], target.at[landing],
            s_send.at[kind, there], s_recv.at[kind, landing], (chan, there),
        )

    def res_copy(kind, there, landing):
        source, target = ((res_pair, out_pair), (res_lone, out_lone))[kind]
        return remote(
            source.at[there], target.at[landing],
            r_send.at[kind, there], r_recv.at[kind, landing], (chan, there),
        )

    def taps_of(at):
        return w_hbm.at[:, pl.ds(pl.multiple_of(at * width, width), width)]

    def tap_copy(there, landing):
        return remote(
            taps_of(there), in_tap.at[landing], t_send.at[there], t_recv.at[landing], (there, seq)
        )

    def back_copy(there, landing):
        return remote(
            out_lone.at[:, there], out_tap.at[landing], b_send.at[there], b_recv.at[landing],
            (there, seq),
        )

    def own_copy(source, target, index):
        return pltpu.make_async_copy(source, target, own_sem.at[index])

    own_sig = [
        own_copy(send_pair.at[seq], in_pair.at[seq], 0), own_copy(send_lone.at[seq], in_lone.at[seq], 1)
    ]
    own_res = [
        own_copy(res_pair.at[seq], out_pair.at[seq], 2), own_copy(res_lone.at[seq], out_lone.at[seq], 3)
    ]
    own_taps = own_copy(taps_of(chan), in_tap.at[chan], 4)
    own_back = own_copy(out_lone.at[:, chan], out_tap.at[chan], 5)
    own_taps.start()

    def pack(slot, pick):
        for u in range(pieces):
            flipped = pick(u).T
            for t in range(n_seq):
                at_slot(send_pair, send_lone, slot, t, u)[...] = flipped[t * group : (t + 1) * group].astype(BF16)

    def product(a_ref, b_ref):
        def pick(u):
            rows = pl.ds(u * fast, fast)
            return a_ref[rows, :].astype(F32) * b_ref[rows, :].astype(F32)

        return pick

    def send(kind):
        others(lambda i: sig_copy(kind, i, seq).start(), seq, n_seq)
        own_sig[kind].start()

    def send_first(i):
        sig_copy(PAIR, i, seq).start()

    def send_tap(i):
        pl.semaphore_wait(chan_ready.at[i], 1)
        tap_copy(i, chan).start()

    loads[0].wait()
    loads[1].wait()
    pack(X, product(k_ref, v_ref))
    loads[2].wait()
    loads[3].wait()
    pack(G, product(g_ref, q_ref))
    pl.semaphore_wait(barrier, n_seq - 1 + chan)
    span(0, chan, lambda i: tell(chan_ready.at[chan], (i, seq)))
    span(0, chan, lambda i: tap_copy(i, chan).start())
    others(send_first, seq, n_seq)
    own_sig[PAIR].start()
    span(chan + 1, n_chan, send_tap)
    for copy in const_loads:
        copy.start()
    own_taps.wait()
    others(lambda i: tap_copy(i, i).wait(), chan, n_chan)
    pack(F, lambda u: in_tap[u].astype(F32))
    send(LONE)
    for copy in const_loads:
        copy.wait()

    cosine, sine = twid_ref[0], twid_ref[1]
    batch = joined(fast, group)

    def times(table, columns):
        if batch == 1:
            return [dot(table, column) for column in columns]
        wide = dot(table, jnp.concatenate(columns, axis=1))
        return [wide[:, i * fast : (i + 1) * fast] for i in range(len(columns))]

    def through(target, slot, table, fine):
        x = short[slot]
        if fine:
            target[slot] = dot(jnp.concatenate([x, x], axis=1), table[...])
        else:
            target[slot] = dot(x, table[: 2 * fast, :])

    def forward(slots):
        for s in range(n_seq):
            for u in range(pieces):
                at = pl.ds((s * pieces + u) * group, group)
                for slot in slots:
                    lines[slot, at, :] = at_slot(in_pair, in_lone, slot, s, u)[...].astype(F32)
        for base in range(0, group, batch):
            for slot in slots:
                columns = []
                for c in range(base, base + batch):
                    column = lines[slot, pl.ds(c, slow, stride=group), :].astype(BF16)
                    columns.append(jnp.concatenate([column, column], axis=0))
                rows = []
                for got in times(first_ref[...], columns):
                    real, imag = got[:padded], got[padded:]
                    rows.append(
                        jnp.concatenate([real * cosine - imag * sine, real * sine + imag * cosine], axis=1)
                    )
                at = pl.ds(base * padded, batch * padded)
                short[slot, at, :] = jnp.concatenate(rows, axis=0).astype(BF16)
        for slot in slots:
            through(turned, slot, ahead_ref, slot != F)

    def inverse(jobs):
        for base in range(0, group, batch):
            at = pl.ds(base * padded, batch * padded)
            for slot, a, b, conjugate in jobs:
                ar, ai = turned[a, at, :fast], turned[a, at, fast:]
                br, bi = turned[b, at, :fast], turned[b, at, fast:]
                if conjugate:
                    real, imag = ar * br + ai * bi, ar * bi - ai * br
                else:
                    real, imag = ar * br - ai * bi, ar * bi + ai * br
                short[slot, at, :] = jnp.concatenate([real, imag], axis=1).astype(BF16)
        for slot, *_ in jobs:
            through(spec, slot, back_ref, slot == GRAD)
        for base in range(0, group, batch):
            for slot, *_ in jobs:
                columns = []
                for c in range(base, base + batch):
                    at = pl.ds(c * padded, padded)
                    real, imag = spec[slot, at, :fast], spec[slot, at, fast:]
                    real, imag = real * cosine + imag * sine, imag * cosine - real * sine
                    both = jnp.concatenate([real, imag], axis=0).astype(BF16)
                    columns.append(jnp.concatenate([both, both], axis=0))
                for c, got in zip(range(base, base + batch), times(last_ref[...], columns)):
                    lines[slot, pl.ds(c, slow, stride=group), :] = got
        for s in range(n_seq):
            for u in range(pieces):
                at = pl.ds((s * pieces + u) * group, group)
                for slot, *_ in jobs:
                    at_slot(res_pair, res_lone, slot, s, u)[...] = lines[slot, at, :].astype(BF16)

    def landed(kind):
        own_sig[kind].wait()
        others(lambda i: sig_copy(kind, i, i).wait(), seq, n_seq)

    def reply(kind):
        others(lambda i: res_copy(kind, i, seq).start(), seq, n_seq)
        own_res[kind].start()

    def arrive(kind):
        own_res[kind].wait()
        others(lambda i: res_copy(kind, i, i).wait(), seq, n_seq)

    landed(PAIR)
    forward((X, G))
    inverse(((GRAD, X, G, True),))
    reply(LONE)
    landed(LONE)
    forward((F,))
    inverse(((Y, F, X, False), (BACK, F, G, True)))
    reply(PAIR)
    arrive(LONE)
    others(lambda i: back_copy(i, chan).start(), chan, n_chan)
    own_back.start()
    arrive(PAIR)
    own_back.wait()
    loads[4].wait()
    others(lambda i: back_copy(i, i).wait(), chan, n_chan)


def after_kernel(
    q_ref, k_ref, v_ref, g_ref, gain_ref, sig_ref, tap_ref, m_ref, qg_ref, kg_ref, vg_ref, fg_ref, hold
):
    seq_parts, _, pieces, group, fast = sig_ref.shape
    gain = gain_ref[...]

    def columns(pick):
        for t in range(seq_parts):
            hold[pl.ds(t * group, group), :] = pick(t).astype(F32)
        return hold[...].T

    for u in range(pieces):
        rows = pl.ds(u * fast, fast)
        query, key = q_ref[rows, :].astype(F32), k_ref[rows, :].astype(F32)
        value, grad = v_ref[rows, :].astype(F32), g_ref[rows, :].astype(F32)
        state = columns(lambda t: sig_ref[t, Y, u]) + gain * (key * value)
        m_ref[rows, :] = (query * state).astype(BF16)
        qg_ref[rows, :] = (grad * state).astype(BF16)
        back = columns(lambda t: sig_ref[t, BACK, u]) + gain * (grad * query)
        kg_ref[rows, :] = (back * value).astype(BF16)
        vg_ref[rows, :] = (back * key).astype(BF16)
    for a in range(pieces):
        got = columns(lambda t: tap_ref[a, t])
        fg_ref[pl.ds(a, fast, stride=pieces), :] = got


def body(n_chan, n_seq, query, key, value, filter_weights, skip_gain, cotangent):
    rows, width = query.shape
    tap_rows, _, all_width = filter_weights.shape
    fast, group, pieces = tap_rows, width // n_seq, n_chan
    slow = rows * n_seq // fast
    padded, first, twiddle, ahead, back, last = tables(
        slow, fast, 1.0 / math.sqrt(rows * n_seq), 16 // joined(fast, group)
    )
    weights = filter_weights.reshape(tap_rows, all_width)
    consts = [
        jnp.concatenate(split_table(first), axis=1),
        jnp.asarray(twiddle, F32),
        jnp.concatenate(split_table(ahead), axis=0),
        jnp.concatenate(split_table(back), axis=0),
        jnp.concatenate(split_table(last), axis=1),
    ]
    pair_dims = (n_seq, 2, pieces, group, fast)
    lone_dims = (n_seq, pieces, group, fast)
    tap_dims = (n_chan, n_seq, group, fast)
    flat_dims = (rows, width)
    dma = pltpu.SemaphoreType.DMA
    anywhere = pl.BlockSpec(memory_space=pl.ANY)
    vmem = pl.BlockSpec(memory_space=pltpu.VMEM)
    sig, taps, gain = pl.pallas_call(
        functools.partial(core_kernel, n_chan, n_seq, padded, len(consts)),
        out_shape=[pltpu.VMEM(pair_dims, BF16), pltpu.VMEM(tap_dims, BF16), pltpu.VMEM((1, width), F32)],
        in_specs=[anywhere] * (6 + len(consts)),
        out_specs=[vmem] * 3,
        scratch_shapes=[
            *[pltpu.VMEM(flat_dims, BF16)] * 4,
            pltpu.VMEM((n_chan, tap_rows, width), BF16),
            *[pltpu.VMEM(pair_dims, BF16)] * 3,
            *[pltpu.VMEM(lone_dims, BF16)] * 4,
            pltpu.VMEM((3, slow * group, fast), F32),
            pltpu.VMEM((3, group * padded, 2 * fast), BF16),
            pltpu.VMEM((3, group * padded, 2 * fast), F32),
            pltpu.VMEM((3, group * padded, 2 * fast), F32),
            *[pltpu.VMEM(const.shape, const.dtype) for const in consts],
            dma((5,)),
            dma((len(consts),)),
            dma((6,)),
            dma((2, n_seq)),
            dma((2, n_seq)),
            dma((n_chan,)),
            dma((n_chan,)),
            dma((2, n_seq)),
            dma((2, n_seq)),
            dma((n_chan,)),
            dma((n_chan,)),
            pltpu.SemaphoreType.REGULAR((n_seq,)),
            pltpu.SemaphoreType.REGULAR((n_chan,)),
        ],
        compiler_params=pltpu.CompilerParams(
            collective_id=0, has_side_effects=True, vmem_limit_bytes=60 * 1024 * 1024
        ),
        name="core",
    )(query, key, value, cotangent, weights, skip_gain.reshape(1, width), *consts)
    flat = jax.ShapeDtypeStruct(flat_dims, BF16)
    outs = pl.pallas_call(
        after_kernel,
        out_shape=[flat, flat, flat, flat, jax.ShapeDtypeStruct((tap_rows * n_chan, width), F32)],
        in_specs=[vmem] * 7,
        out_specs=[vmem] * 5,
        scratch_shapes=[pltpu.VMEM((width, fast), F32)],
        compiler_params=pltpu.CompilerParams(vmem_limit_bytes=24 * 1024 * 1024),
        name="after",
    )(query, key, value, cotangent, gain, sig, taps)
    return (*outs[:4], outs[4].reshape(tap_rows, 1, all_width))


def solution(mesh):
    n_chan, n_seq = mesh.shape["chan"], mesh.shape["seq"]
    block = P("seq", "chan")
    taps = P("chan", "seq", None)
    return jax.shard_map(
        functools.partial(body, n_chan, n_seq),
        mesh=mesh,
        in_specs=(block, block, block, taps, P("chan"), block),
        out_specs=(block, block, block, block, taps),
        check_vma=False,
    )
```

```python
import functools
import math

import jax
import jax.numpy as jnp
import numpy as np
from jax import lax
from jax.experimental import pallas as pl
from jax.experimental.pallas import tpu as pltpu
from jax.sharding import PartitionSpec as P

MESH = pl.DeviceIdType.MESH
F32 = jnp.float32
BF16 = jnp.bfloat16
X, G, F = 0, 1, 2
Y, BACK, GRAD = 0, 1, 2
PAIR, LONE = 0, 1


def split_table(table):
    high = jnp.asarray(table, F32).astype(BF16)
    low = (jnp.asarray(table, F32) - high.astype(F32)).astype(BF16)
    return high, low


def dot(a, b):
    return jnp.dot(a, b, preferred_element_type=F32)


def tables(slow, fast, factor, tile):
    length = 2 * slow * fast
    kept = slow + 1
    padded = -(-kept // tile) * tile
    k1 = np.arange(kept)
    n1 = np.arange(slow)
    n2 = np.arange(fast)
    angle1 = 2.0 * np.pi * (np.outer(k1, n1) % (2 * slow)) / (2 * slow)
    first = np.zeros((2 * padded, slow))
    first[:kept] = np.cos(angle1)
    first[padded : padded + kept] = -np.sin(angle1)
    angle2 = 2.0 * np.pi * (np.outer(k1, n2) % length) / length
    twiddle = np.zeros((2, padded, fast))
    twiddle[0, :kept] = np.cos(angle2)
    twiddle[1, :kept] = -np.sin(angle2)
    angle3 = 2.0 * np.pi * (np.outer(n2, n2) % fast) / fast
    cosine, sine = np.cos(angle3), np.sin(angle3)
    ahead = np.block([[cosine, -sine], [sine, cosine]])
    back = np.block([[cosine, sine], [-sine, cosine]])
    weight = np.where((k1 == 0) | (k1 == slow), 1.0, 2.0)[:, None] * (factor / length)
    last = np.zeros((slow, 2 * padded))
    last[:, :kept] = (weight * np.cos(angle1)).T
    last[:, padded : padded + kept] = (-weight * np.sin(angle1)).T
    return padded, first, twiddle, ahead, back, last


def joined(fast, group):
    return 2 if fast % 128 == 0 and group % 2 == 0 else 1


def core_kernel(n_chan, n_seq, padded, n_const, *refs):
    q_hbm, k_hbm, v_hbm, g_hbm, w_hbm, gain_hbm = refs[:6]
    const_hbm = refs[6 : 6 + n_const]
    out_pair, out_tap, out_gain = refs[6 + n_const : 9 + n_const]
    (
        q_ref, k_ref, v_ref, g_ref, in_tap, send_pair, in_pair, res_pair, send_lone, in_lone, res_lone, out_lone,
        lines, short, turned, spec,
    ) = refs[9 + n_const : 25 + n_const]
    consts = refs[25 + n_const : 25 + 2 * n_const]
    (
        load_sem, const_sem, own_sem, s_send, s_recv, t_send, t_recv, r_send, r_recv, b_send, b_recv,
        chan_ready,
    ) = refs[25 + 2 * n_const :]
    first_ref, twid_ref, ahead_ref, back_ref, last_ref = consts
    chan, seq = lax.axis_index("chan"), lax.axis_index("seq")
    _, pieces, group, fast = send_lone.shape
    slow = n_seq * pieces
    width = n_seq * group

    def each(count, act):
        def step(d, carry):
            act(d)
            return carry

        lax.fori_loop(1, count, step, 0)

    barrier = pltpu.get_barrier_semaphore()

    def greet(device):
        pl.semaphore_signal(barrier, inc=1, device_id=device, device_id_type=MESH)

    def tell(ready, device):
        pl.semaphore_signal(ready, inc=1, device_id=device, device_id_type=MESH)

    def span(low, high, act):
        def step(i, carry):
            act(i)
            return carry

        lax.fori_loop(low, high, step, 0)

    def pairwise(act):
        if n_seq & (n_seq - 1):
            others(act, seq, n_seq)
            return
        half = n_seq // 2
        for far in range(n_seq - 1, half - 1, -1):
            act(jnp.bitwise_xor(seq, far))
            if far > half:
                act(jnp.bitwise_xor(seq, far - half))

    def others(act, own, count):
        each(count, lambda d: act(lax.rem(own + d, count)))

    loads = [
        pltpu.make_async_copy(source, target, load_sem.at[i])
        for i, (source, target) in enumerate(
            [(k_hbm, k_ref), (v_hbm, v_ref), (g_hbm, g_ref), (q_hbm, q_ref), (gain_hbm, out_gain)]
        )
    ]
    for copy in loads[:2]:
        copy.start()
    others(lambda i: greet((chan, i)), seq, n_seq)
    span(chan + 1, n_chan, lambda i: greet((i, seq)))
    for copy in loads[2:]:
        copy.start()
    const_loads = [
        pltpu.make_async_copy(source, target, const_sem.at[i])
        for i, (source, target) in enumerate(zip(const_hbm, consts))
    ]

    def remote(source, target, send, recv, device):
        return pltpu.make_async_remote_copy(
            src_ref=source, dst_ref=target, send_sem=send, recv_sem=recv,
            device_id=device, device_id_type=MESH,
        )

    def at_slot(pair, lone, slot, peer, u):
        return lone.at[peer, u] if slot == 2 else pair.at[peer, slot, u]

    def sig_copy(kind, there, landing):
        source, target = ((send_pair, in_pair), (send_lone, in_lone))[kind]
        return remote(
            source.at[there], target.at[landing],
            s_send.at[kind, there], s_recv.at[kind, landing], (chan, there),
        )

    def res_copy(kind, there, landing):
        source, target = ((res_pair, out_pair), (res_lone, out_lone))[kind]
        return remote(
            source.at[there], target.at[landing],
            r_send.at[kind, there], r_recv.at[kind, landing], (chan, there),
        )

    def taps_of(at):
        return w_hbm.at[:, pl.ds(pl.multiple_of(at * width, width), width)]

    def tap_copy(there, landing):
        return remote(
            taps_of(there), in_tap.at[landing], t_send.at[there], t_recv.at[landing], (there, seq)
        )

    def back_copy(there, landing):
        return remote(
            out_lone.at[:, there], out_tap.at[landing], b_send.at[there], b_recv.at[landing],
            (there, seq),
        )

    def own_copy(source, target, index):
        return pltpu.make_async_copy(source, target, own_sem.at[index])

    own_sig = [
        own_copy(send_pair.at[seq], in_pair.at[seq], 0), own_copy(send_lone.at[seq], in_lone.at[seq], 1)
    ]
    own_res = [
        own_copy(res_pair.at[seq], out_pair.at[seq], 2), own_copy(res_lone.at[seq], out_lone.at[seq], 3)
    ]
    own_taps = own_copy(taps_of(chan), in_tap.at[chan], 4)
    own_back = own_copy(out_lone.at[:, chan], out_tap.at[chan], 5)
    own_taps.start()

    def pack(slot, pick):
        for u in range(pieces):
            flipped = pick(u).T
            for t in range(n_seq):
                at_slot(send_pair, send_lone, slot, t, u)[...] = flipped[t * group : (t + 1) * group].astype(BF16)

    def product(a_ref, b_ref):
        def pick(u):
            rows = pl.ds(u * fast, fast)
            return a_ref[rows, :].astype(F32) * b_ref[rows, :].astype(F32)

        return pick

    def send_tap(i):
        pl.semaphore_wait(chan_ready.at[i], 1)
        tap_copy(i, chan).start()

    loads[0].wait()
    loads[1].wait()
    pack(X, product(k_ref, v_ref))
    loads[2].wait()
    loads[3].wait()
    pack(G, product(g_ref, q_ref))
    pl.semaphore_wait(barrier, n_seq - 1 + chan)
    span(0, chan, lambda i: tell(chan_ready.at[chan], (i, seq)))
    span(0, chan, lambda i: tap_copy(i, chan).start())
    pairwise(lambda i: sig_copy(PAIR, i, seq).start())
    own_sig[PAIR].start()
    span(chan + 1, n_chan, send_tap)
    for copy in const_loads:
        copy.start()
    own_taps.wait()
    others(lambda i: tap_copy(i, i).wait(), chan, n_chan)
    pack(F, lambda u: in_tap[u].astype(F32))
    pairwise(lambda i: sig_copy(LONE, i, seq).start())
    own_sig[LONE].start()
    for copy in const_loads:
        copy.wait()

    cosine, sine = twid_ref[0], twid_ref[1]
    batch = joined(fast, group)

    def times(table, columns):
        if batch == 1:
            return [dot(table, column) for column in columns]
        wide = dot(table, jnp.concatenate(columns, axis=1))
        return [wide[:, i * fast : (i + 1) * fast] for i in range(len(columns))]

    def through(target, slot, table, fine):
        x = short[slot]
        if fine:
            target[slot] = dot(jnp.concatenate([x, x], axis=1), table[...])
        else:
            target[slot] = dot(x, table[: 2 * fast, :])

    def forward(slots):
        for s in range(n_seq):
            for u in range(pieces):
                at = pl.ds((s * pieces + u) * group, group)
                for slot in slots:
                    lines[slot, at, :] = at_slot(in_pair, in_lone, slot, s, u)[...].astype(F32)
        for base in range(0, group, batch):
            for slot in slots:
                columns = []
                for c in range(base, base + batch):
                    column = lines[slot, pl.ds(c, slow, stride=group), :].astype(BF16)
                    columns.append(jnp.concatenate([column, column], axis=0))
                rows = []
                for got in times(first_ref[...], columns):
                    real, imag = got[:padded], got[padded:]
                    rows.append(
                        jnp.concatenate([real * cosine - imag * sine, real * sine + imag * cosine], axis=1)
                    )
                at = pl.ds(base * padded, batch * padded)
                short[slot, at, :] = jnp.concatenate(rows, axis=0).astype(BF16)
        for slot in slots:
            through(turned, slot, ahead_ref, slot != F)

    def inverse(jobs):
        for base in range(0, group, batch):
            at = pl.ds(base * padded, batch * padded)
            for slot, a, b, conjugate in jobs:
                ar, ai = turned[a, at, :fast], turned[a, at, fast:]
                br, bi = turned[b, at, :fast], turned[b, at, fast:]
                if conjugate:
                    real, imag = ar * br + ai * bi, ar * bi - ai * br
                else:
                    real, imag = ar * br - ai * bi, ar * bi + ai * br
                short[slot, at, :] = jnp.concatenate([real, imag], axis=1).astype(BF16)
        for slot, *_ in jobs:
            through(spec, slot, back_ref, slot == GRAD)
        for base in range(0, group, batch):
            for slot, *_ in jobs:
                columns = []
                for c in range(base, base + batch):
                    at = pl.ds(c * padded, padded)
                    real, imag = spec[slot, at, :fast], spec[slot, at, fast:]
                    real, imag = real * cosine + imag * sine, imag * cosine - real * sine
                    both = jnp.concatenate([real, imag], axis=0).astype(BF16)
                    columns.append(jnp.concatenate([both, both], axis=0))
                for c, got in zip(range(base, base + batch), times(last_ref[...], columns)):
                    lines[slot, pl.ds(c, slow, stride=group), :] = got
        for s in range(n_seq):
            for u in range(pieces):
                at = pl.ds((s * pieces + u) * group, group)
                for slot, *_ in jobs:
                    at_slot(res_pair, res_lone, slot, s, u)[...] = lines[slot, at, :].astype(BF16)

    def landed(kind):
        own_sig[kind].wait()
        others(lambda i: sig_copy(kind, i, i).wait(), seq, n_seq)

    def reply(kind):
        others(lambda i: res_copy(kind, i, seq).start(), seq, n_seq)
        own_res[kind].start()

    def arrive(kind):
        own_res[kind].wait()
        others(lambda i: res_copy(kind, i, i).wait(), seq, n_seq)

    landed(PAIR)
    forward((X, G))
    inverse(((GRAD, X, G, True),))
    reply(LONE)
    landed(LONE)
    forward((F,))
    inverse(((Y, F, X, False), (BACK, F, G, True)))
    reply(PAIR)
    arrive(LONE)
    others(lambda i: back_copy(i, chan).start(), chan, n_chan)
    own_back.start()
    arrive(PAIR)
    own_back.wait()
    loads[4].wait()
    others(lambda i: back_copy(i, i).wait(), chan, n_chan)


def after_kernel(
    q_ref, k_ref, v_ref, g_ref, gain_ref, sig_ref, tap_ref, m_ref, qg_ref, kg_ref, vg_ref, fg_ref, hold
):
    seq_parts, _, pieces, group, fast = sig_ref.shape
    gain = gain_ref[...]

    def columns(pick):
        for t in range(seq_parts):
            hold[pl.ds(t * group, group), :] = pick(t).astype(F32)
        return hold[...].T

    for u in range(pieces):
        rows = pl.ds(u * fast, fast)
        query, key = q_ref[rows, :].astype(F32), k_ref[rows, :].astype(F32)
        value, grad = v_ref[rows, :].astype(F32), g_ref[rows, :].astype(F32)
        state = columns(lambda t: sig_ref[t, Y, u]) + gain * (key * value)
        m_ref[rows, :] = (query * state).astype(BF16)
        qg_ref[rows, :] = (grad * state).astype(BF16)
        back = columns(lambda t: sig_ref[t, BACK, u]) + gain * (grad * query)
        kg_ref[rows, :] = (back * value).astype(BF16)
        vg_ref[rows, :] = (back * key).astype(BF16)
    for a in range(pieces):
        got = columns(lambda t: tap_ref[a, t])
        fg_ref[pl.ds(a, fast, stride=pieces), :] = got


def body(n_chan, n_seq, query, key, value, filter_weights, skip_gain, cotangent):
    rows, width = query.shape
    tap_rows, _, all_width = filter_weights.shape
    fast, group, pieces = tap_rows, width // n_seq, n_chan
    slow = rows * n_seq // fast
    padded, first, twiddle, ahead, back, last = tables(
        slow, fast, 1.0 / math.sqrt(rows * n_seq), 16 // joined(fast, group)
    )
    weights = filter_weights.reshape(tap_rows, all_width)
    consts = [
        jnp.concatenate(split_table(first), axis=1),
        jnp.asarray(twiddle, F32),
        jnp.concatenate(split_table(ahead), axis=0),
        jnp.concatenate(split_table(back), axis=0),
        jnp.concatenate(split_table(last), axis=1),
    ]
    pair_dims = (n_seq, 2, pieces, group, fast)
    lone_dims = (n_seq, pieces, group, fast)
    tap_dims = (n_chan, n_seq, group, fast)
    flat_dims = (rows, width)
    dma = pltpu.SemaphoreType.DMA
    anywhere = pl.BlockSpec(memory_space=pl.ANY)
    vmem = pl.BlockSpec(memory_space=pltpu.VMEM)
    sig, taps, gain = pl.pallas_call(
        functools.partial(core_kernel, n_chan, n_seq, padded, len(consts)),
        out_shape=[pltpu.VMEM(pair_dims, BF16), pltpu.VMEM(tap_dims, BF16), pltpu.VMEM((1, width), F32)],
        in_specs=[anywhere] * (6 + len(consts)),
        out_specs=[vmem] * 3,
        scratch_shapes=[
            *[pltpu.VMEM(flat_dims, BF16)] * 4,
            pltpu.VMEM((n_chan, tap_rows, width), BF16),
            *[pltpu.VMEM(pair_dims, BF16)] * 3,
            *[pltpu.VMEM(lone_dims, BF16)] * 4,
            pltpu.VMEM((3, slow * group, fast), F32),
            pltpu.VMEM((3, group * padded, 2 * fast), BF16),
            pltpu.VMEM((3, group * padded, 2 * fast), F32),
            pltpu.VMEM((3, group * padded, 2 * fast), F32),
            *[pltpu.VMEM(const.shape, const.dtype) for const in consts],
            dma((5,)),
            dma((len(consts),)),
            dma((6,)),
            dma((2, n_seq)),
            dma((2, n_seq)),
            dma((n_chan,)),
            dma((n_chan,)),
            dma((2, n_seq)),
            dma((2, n_seq)),
            dma((n_chan,)),
            dma((n_chan,)),
            pltpu.SemaphoreType.REGULAR((n_chan,)),
        ],
        compiler_params=pltpu.CompilerParams(
            collective_id=0, has_side_effects=True, vmem_limit_bytes=60 * 1024 * 1024
        ),
        name="core",
    )(query, key, value, cotangent, weights, skip_gain.reshape(1, width), *consts)
    flat = jax.ShapeDtypeStruct(flat_dims, BF16)
    outs = pl.pallas_call(
        after_kernel,
        out_shape=[flat, flat, flat, flat, jax.ShapeDtypeStruct((tap_rows * n_chan, width), F32)],
        in_specs=[vmem] * 7,
        out_specs=[vmem] * 5,
        scratch_shapes=[pltpu.VMEM((width, fast), F32)],
        compiler_params=pltpu.CompilerParams(vmem_limit_bytes=24 * 1024 * 1024),
        name="after",
    )(query, key, value, cotangent, gain, sig, taps)
    return (*outs[:4], outs[4].reshape(tap_rows, 1, all_width))


def solution(mesh):
    n_chan, n_seq = mesh.shape["chan"], mesh.shape["seq"]
    block = P("seq", "chan")
    taps = P("chan", "seq", None)
    return jax.shard_map(
        functools.partial(body, n_chan, n_seq),
        mesh=mesh,
        in_specs=(block, block, block, taps, P("chan"), block),
        out_specs=(block, block, block, block, taps),
        check_vma=False,
    )
```

```python
import functools
import math

import jax
import jax.numpy as jnp
import numpy as np
from jax import lax
from jax.experimental import pallas as pl
from jax.experimental.pallas import tpu as pltpu
from jax.sharding import PartitionSpec as P

MESH = pl.DeviceIdType.MESH
F32 = jnp.float32
BF16 = jnp.bfloat16
X, G, F = 0, 1, 2
Y, BACK, GRAD = 0, 1, 2
PAIR, LONE = 0, 1


def split_table(table):
    high = jnp.asarray(table, F32).astype(BF16)
    low = (jnp.asarray(table, F32) - high.astype(F32)).astype(BF16)
    return high, low


def dot(a, b):
    return jnp.dot(a, b, preferred_element_type=F32)


def tables(slow, fast, factor, tile):
    length = 2 * slow * fast
    kept = slow + 1
    padded = -(-kept // tile) * tile
    k1 = np.arange(kept)
    n1 = np.arange(slow)
    n2 = np.arange(fast)
    angle1 = 2.0 * np.pi * (np.outer(k1, n1) % (2 * slow)) / (2 * slow)
    first = np.zeros((2 * padded, slow))
    first[:kept] = np.cos(angle1)
    first[padded : padded + kept] = -np.sin(angle1)
    angle2 = 2.0 * np.pi * (np.outer(k1, n2) % length) / length
    twiddle = np.zeros((2, padded, fast))
    twiddle[0, :kept] = np.cos(angle2)
    twiddle[1, :kept] = -np.sin(angle2)
    angle3 = 2.0 * np.pi * (np.outer(n2, n2) % fast) / fast
    cosine, sine = np.cos(angle3), np.sin(angle3)
    ahead = np.block([[cosine, -sine], [sine, cosine]])
    back = np.block([[cosine, sine], [-sine, cosine]])
    weight = np.where((k1 == 0) | (k1 == slow), 1.0, 2.0)[:, None] * (factor / length)
    last = np.zeros((slow, 2 * padded))
    last[:, :kept] = (weight * np.cos(angle1)).T
    last[:, padded : padded + kept] = (-weight * np.sin(angle1)).T
    return padded, first, twiddle, ahead, back, last


def joined(fast, group):
    return 2 if fast % 128 == 0 and group % 2 == 0 else 1


def core_kernel(n_chan, n_seq, padded, n_const, *refs):
    q_hbm, k_hbm, v_hbm, g_hbm, w_hbm, gain_hbm = refs[:6]
    const_hbm = refs[6 : 6 + n_const]
    out_pair, out_grad, out_gain = refs[6 + n_const : 9 + n_const]
    (
        q_ref, k_ref, v_ref, g_ref, in_tap, send_pair, in_pair, res_pair, send_lone, in_lone, res_lone, out_lone,
        lines, short, turned, spec, out_tap, hold,
    ) = refs[9 + n_const : 27 + n_const]
    consts = refs[27 + n_const : 27 + 2 * n_const]
    (
        load_sem, const_sem, own_sem, s_send, s_recv, t_send, t_recv, r_send, r_recv, b_send, b_recv,
        chan_ready,
    ) = refs[27 + 2 * n_const :]
    first_ref, twid_ref, ahead_ref, back_ref, last_ref = consts
    chan, seq = lax.axis_index("chan"), lax.axis_index("seq")
    _, pieces, group, fast = send_lone.shape
    slow = n_seq * pieces
    width = n_seq * group

    def each(count, act):
        def step(d, carry):
            act(d)
            return carry

        lax.fori_loop(1, count, step, 0)

    barrier = pltpu.get_barrier_semaphore()

    def greet(device):
        pl.semaphore_signal(barrier, inc=1, device_id=device, device_id_type=MESH)

    def tell(ready, device):
        pl.semaphore_signal(ready, inc=1, device_id=device, device_id_type=MESH)

    def span(low, high, act):
        def step(i, carry):
            act(i)
            return carry

        lax.fori_loop(low, high, step, 0)

    def pairwise(act):
        if n_seq & (n_seq - 1):
            others(act, seq, n_seq)
            return
        half = n_seq // 2
        for far in range(n_seq - 1, half - 1, -1):
            act(jnp.bitwise_xor(seq, far))
            if far > half:
                act(jnp.bitwise_xor(seq, far - half))

    def others(act, own, count):
        each(count, lambda d: act(lax.rem(own + d, count)))

    loads = [
        pltpu.make_async_copy(source, target, load_sem.at[i])
        for i, (source, target) in enumerate(
            [(k_hbm, k_ref), (v_hbm, v_ref), (g_hbm, g_ref), (q_hbm, q_ref), (gain_hbm, out_gain)]
        )
    ]
    for copy in loads[:2]:
        copy.start()
    others(lambda i: greet((chan, i)), seq, n_seq)
    span(chan + 1, n_chan, lambda i: greet((i, seq)))
    for copy in loads[2:]:
        copy.start()
    const_loads = [
        pltpu.make_async_copy(source, target, const_sem.at[i])
        for i, (source, target) in enumerate(zip(const_hbm, consts))
    ]

    def remote(source, target, send, recv, device):
        return pltpu.make_async_remote_copy(
            src_ref=source, dst_ref=target, send_sem=send, recv_sem=recv,
            device_id=device, device_id_type=MESH,
        )

    def at_slot(pair, lone, slot, peer, u):
        return lone.at[peer, u] if slot == 2 else pair.at[peer, slot, u]

    def sig_copy(kind, there, landing):
        source, target = ((send_pair, in_pair), (send_lone, in_lone))[kind]
        return remote(
            source.at[there], target.at[landing],
            s_send.at[kind, there], s_recv.at[kind, landing], (chan, there),
        )

    def res_copy(kind, there, landing):
        source, target = ((res_pair, out_pair), (res_lone, out_lone))[kind]
        return remote(
            source.at[there], target.at[landing],
            r_send.at[kind, there], r_recv.at[kind, landing], (chan, there),
        )

    def taps_of(at):
        return w_hbm.at[:, pl.ds(pl.multiple_of(at * width, width), width)]

    def tap_copy(there, landing):
        return remote(
            taps_of(there), in_tap.at[landing], t_send.at[there], t_recv.at[landing], (there, seq)
        )

    def back_copy(there, landing):
        return remote(
            out_lone.at[:, there], out_tap.at[landing], b_send.at[there], b_recv.at[landing],
            (there, seq),
        )

    def own_copy(source, target, index):
        return pltpu.make_async_copy(source, target, own_sem.at[index])

    own_sig = [
        own_copy(send_pair.at[seq], in_pair.at[seq], 0), own_copy(send_lone.at[seq], in_lone.at[seq], 1)
    ]
    own_res = [
        own_copy(res_pair.at[seq], out_pair.at[seq], 2), own_copy(res_lone.at[seq], out_lone.at[seq], 3)
    ]
    own_taps = own_copy(taps_of(chan), in_tap.at[chan], 4)
    own_back = own_copy(out_lone.at[:, chan], out_tap.at[chan], 5)
    own_taps.start()

    def pack(slot, pick):
        for u in range(pieces):
            flipped = pick(u).T
            for t in range(n_seq):
                at_slot(send_pair, send_lone, slot, t, u)[...] = flipped[t * group : (t + 1) * group].astype(BF16)

    def product(a_ref, b_ref):
        def pick(u):
            rows = pl.ds(u * fast, fast)
            return a_ref[rows, :].astype(F32) * b_ref[rows, :].astype(F32)

        return pick

    def send_tap(i):
        pl.semaphore_wait(chan_ready.at[i], 1)
        tap_copy(i, chan).start()

    loads[0].wait()
    loads[1].wait()
    pack(X, product(k_ref, v_ref))
    loads[2].wait()
    loads[3].wait()
    pack(G, product(g_ref, q_ref))
    pl.semaphore_wait(barrier, n_seq - 1 + chan)
    span(0, chan, lambda i: tell(chan_ready.at[chan], (i, seq)))
    own_sig[PAIR].start()
    pairwise(lambda i: sig_copy(PAIR, i, seq).start())
    span(0, chan, lambda i: tap_copy(i, chan).start())
    span(chan + 1, n_chan, send_tap)
    for copy in const_loads:
        copy.start()
    own_taps.wait()
    others(lambda i: tap_copy(i, i).wait(), chan, n_chan)
    pack(F, lambda u: in_tap[u].astype(F32))
    own_sig[LONE].start()
    pairwise(lambda i: sig_copy(LONE, i, seq).start())
    for copy in const_loads:
        copy.wait()

    cosine, sine = twid_ref[0], twid_ref[1]
    batch = joined(fast, group)

    def times(table, columns):
        if batch == 1:
            return [dot(table, column) for column in columns]
        wide = dot(table, jnp.concatenate(columns, axis=1))
        return [wide[:, i * fast : (i + 1) * fast] for i in range(len(columns))]

    def through(target, slot, table):
        x = short[slot]
        target[slot] = dot(jnp.concatenate([x, x], axis=1), table[...])

    def forward(slots):
        for s in range(n_seq):
            for u in range(pieces):
                at = pl.ds((s * pieces + u) * group, group)
                for slot in slots:
                    lines[slot, at, :] = at_slot(in_pair, in_lone, slot, s, u)[...].astype(F32)
        for base in range(0, group, batch):
            for slot in slots:
                columns = []
                for c in range(base, base + batch):
                    column = lines[slot, pl.ds(c, slow, stride=group), :].astype(BF16)
                    columns.append(jnp.concatenate([column, column], axis=0))
                rows = []
                for got in times(first_ref[...], columns):
                    real, imag = got[:padded], got[padded:]
                    rows.append(
                        jnp.concatenate([real * cosine - imag * sine, real * sine + imag * cosine], axis=1)
                    )
                at = pl.ds(base * padded, batch * padded)
                short[slot, at, :] = jnp.concatenate(rows, axis=0).astype(BF16)
        for slot in slots:
            through(turned, slot, ahead_ref)

    def inverse(jobs):
        for base in range(0, group, batch):
            at = pl.ds(base * padded, batch * padded)
            for slot, a, b, conjugate in jobs:
                ar, ai = turned[a, at, :fast], turned[a, at, fast:]
                br, bi = turned[b, at, :fast], turned[b, at, fast:]
                if conjugate:
                    real, imag = ar * br + ai * bi, ar * bi - ai * br
                else:
                    real, imag = ar * br - ai * bi, ar * bi + ai * br
                short[slot, at, :] = jnp.concatenate([real, imag], axis=1).astype(BF16)
        for slot, *_ in jobs:
            through(spec, slot, back_ref)
        for base in range(0, group, batch):
            for slot, *_ in jobs:
                columns = []
                for c in range(base, base + batch):
                    at = pl.ds(c * padded, padded)
                    real, imag = spec[slot, at, :fast], spec[slot, at, fast:]
                    real, imag = real * cosine + imag * sine, imag * cosine - real * sine
                    both = jnp.concatenate([real, imag], axis=0).astype(BF16)
                    columns.append(jnp.concatenate([both, both], axis=0))
                for c, got in zip(range(base, base + batch), times(last_ref[...], columns)):
                    lines[slot, pl.ds(c, slow, stride=group), :] = got
        for s in range(n_seq):
            for u in range(pieces):
                at = pl.ds((s * pieces + u) * group, group)
                for slot, *_ in jobs:
                    at_slot(res_pair, res_lone, slot, s, u)[...] = lines[slot, at, :].astype(BF16)

    def landed(kind):
        own_sig[kind].wait()
        others(lambda i: sig_copy(kind, i, i).wait(), seq, n_seq)

    def reply(kind):
        own_res[kind].start()
        others(lambda i: res_copy(kind, i, seq).start(), seq, n_seq)

    def arrive(kind):
        own_res[kind].wait()
        others(lambda i: res_copy(kind, i, i).wait(), seq, n_seq)

    landed(PAIR)
    forward((X, G))
    inverse(((GRAD, X, G, True),))
    reply(LONE)
    landed(LONE)
    forward((F,))
    inverse(((Y, F, X, False), (BACK, F, G, True)))
    reply(PAIR)
    arrive(LONE)
    others(lambda i: back_copy(i, chan).start(), chan, n_chan)
    own_back.start()
    own_back.wait()
    others(lambda i: back_copy(i, i).wait(), chan, n_chan)
    for a in range(pieces):
        for t in range(n_seq):
            hold[a, pl.ds(t * group, group), :] = out_tap[a, t].astype(F32)
        out_grad[pl.ds(a, fast, stride=pieces), :] = hold[a].T
    loads[4].wait()
    arrive(PAIR)


def after_kernel(
    q_ref, k_ref, v_ref, g_ref, gain_ref, sig_ref, grad_ref, m_hbm, qg_hbm, kg_hbm, vg_hbm, fg_hbm,
    m_ref, qg_ref, kg_ref, vg_ref, hold, sem,
):
    seq_parts, _, pieces, group, fast = sig_ref.shape
    gain = gain_ref[...]
    copies = []

    def write(source, target):
        copies.append(pltpu.make_async_copy(source, target, sem.at[len(copies)]))
        copies[-1].start()

    def columns(slot, u):
        for t in range(seq_parts):
            hold[slot, u, pl.ds(t * group, group), :] = sig_ref[t, slot, u].astype(F32)
        return hold[slot, u].T

    write(grad_ref, fg_hbm)
    for u in range(pieces):
        rows = pl.ds(u * fast, fast)
        query, key = q_ref[rows, :].astype(F32), k_ref[rows, :].astype(F32)
        value, grad = v_ref[rows, :].astype(F32), g_ref[rows, :].astype(F32)
        state = columns(Y, u) + gain * (key * value)
        m_ref[rows, :] = (query * state).astype(BF16)
        qg_ref[rows, :] = (grad * state).astype(BF16)
        back = columns(BACK, u) + gain * (grad * query)
        kg_ref[rows, :] = (back * value).astype(BF16)
        vg_ref[rows, :] = (back * key).astype(BF16)
        for source, target in ((m_ref, m_hbm), (qg_ref, qg_hbm), (kg_ref, kg_hbm), (vg_ref, vg_hbm)):
            write(source.at[rows, :], target.at[rows, :])
    for copy in copies:
        copy.wait()


def body(n_chan, n_seq, query, key, value, filter_weights, skip_gain, cotangent):
    rows, width = query.shape
    tap_rows, _, all_width = filter_weights.shape
    fast, group, pieces = tap_rows, width // n_seq, n_chan
    slow = rows * n_seq // fast
    padded, first, twiddle, ahead, back, last = tables(
        slow, fast, 1.0 / math.sqrt(rows * n_seq), 16 // joined(fast, group)
    )
    weights = filter_weights.reshape(tap_rows, all_width)
    consts = [
        jnp.concatenate(split_table(first), axis=1),
        jnp.asarray(twiddle, F32),
        jnp.concatenate(split_table(ahead), axis=0),
        jnp.concatenate(split_table(back), axis=0),
        jnp.concatenate(split_table(last), axis=1),
    ]
    pair_dims = (n_seq, 2, pieces, group, fast)
    lone_dims = (n_seq, pieces, group, fast)
    tap_dims = (n_chan, n_seq, group, fast)
    flat_dims = (rows, width)
    dma = pltpu.SemaphoreType.DMA
    anywhere = pl.BlockSpec(memory_space=pl.ANY)
    vmem = pl.BlockSpec(memory_space=pltpu.VMEM)
    sig, taps, gain = pl.pallas_call(
        functools.partial(core_kernel, n_chan, n_seq, padded, len(consts)),
        out_shape=[pltpu.VMEM(pair_dims, BF16), pltpu.VMEM((tap_rows * n_chan, width), F32), pltpu.VMEM((1, width), F32)],
        in_specs=[anywhere] * (6 + len(consts)),
        out_specs=[vmem] * 3,
        scratch_shapes=[
            *[pltpu.VMEM(flat_dims, BF16)] * 4,
            pltpu.VMEM((n_chan, tap_rows, width), BF16),
            *[pltpu.VMEM(pair_dims, BF16)] * 3,
            *[pltpu.VMEM(lone_dims, BF16)] * 4,
            pltpu.VMEM((3, slow * group, fast), F32),
            pltpu.VMEM((3, group * padded, 2 * fast), BF16),
            pltpu.VMEM((3, group * padded, 2 * fast), F32),
            pltpu.VMEM((3, group * padded, 2 * fast), F32),
            pltpu.VMEM(tap_dims, BF16),
            pltpu.VMEM((n_chan, width, fast), F32),
            *[pltpu.VMEM(const.shape, const.dtype) for const in consts],
            dma((5,)),
            dma((len(consts),)),
            dma((6,)),
            dma((2, n_seq)),
            dma((2, n_seq)),
            dma((n_chan,)),
            dma((n_chan,)),
            dma((2, n_seq)),
            dma((2, n_seq)),
            dma((n_chan,)),
            dma((n_chan,)),
            pltpu.SemaphoreType.REGULAR((n_chan,)),
        ],
        compiler_params=pltpu.CompilerParams(
            collective_id=0, has_side_effects=True, vmem_limit_bytes=60 * 1024 * 1024
        ),
        name="core",
    )(query, key, value, cotangent, weights, skip_gain.reshape(1, width), *consts)
    flat = jax.ShapeDtypeStruct(flat_dims, BF16)
    outs = pl.pallas_call(
        after_kernel,
        out_shape=[flat, flat, flat, flat, jax.ShapeDtypeStruct((tap_rows * n_chan, width), F32)],
        in_specs=[vmem] * 7,
        out_specs=[anywhere] * 5,
        scratch_shapes=[
            *[pltpu.VMEM(flat_dims, BF16)] * 4,
            pltpu.VMEM((2, pieces, width, fast), F32),
            dma((1 + 4 * pieces,)),
        ],
        compiler_params=pltpu.CompilerParams(vmem_limit_bytes=24 * 1024 * 1024),
        name="after",
    )(query, key, value, cotangent, gain, sig, taps)
    return (*outs[:4], outs[4].reshape(tap_rows, 1, all_width))


def solution(mesh):
    n_chan, n_seq = mesh.shape["chan"], mesh.shape["seq"]
    block = P("seq", "chan")
    taps = P("chan", "seq", None)
    return jax.shard_map(
        functools.partial(body, n_chan, n_seq),
        mesh=mesh,
        in_specs=(block, block, block, taps, P("chan"), block),
        out_specs=(block, block, block, block, taps),
        check_vma=False,
    )
```

```python
import functools
import math

import jax
import jax.numpy as jnp
import numpy as np
from jax import lax
from jax.experimental import pallas as pl
from jax.experimental.pallas import tpu as pltpu
from jax.sharding import PartitionSpec as P

MESH = pl.DeviceIdType.MESH
F32 = jnp.float32
BF16 = jnp.bfloat16
X, G, F = 0, 1, 2
Y, BACK, GRAD = 0, 1, 2
PAIR, LONE = 0, 1


def split_table(table):
    high = jnp.asarray(table, F32).astype(BF16)
    low = (jnp.asarray(table, F32) - high.astype(F32)).astype(BF16)
    return high, low


def dot(a, b):
    return jnp.dot(a, b, preferred_element_type=F32)


def tables(slow, fast, factor, tile):
    length = 2 * slow * fast
    kept = slow + 1
    padded = -(-kept // tile) * tile
    k1 = np.arange(kept)
    n1 = np.arange(slow)
    n2 = np.arange(fast)
    angle1 = 2.0 * np.pi * (np.outer(k1, n1) % (2 * slow)) / (2 * slow)
    first = np.zeros((2 * padded, slow))
    first[:kept] = np.cos(angle1)
    first[padded : padded + kept] = -np.sin(angle1)
    angle2 = 2.0 * np.pi * (np.outer(k1, n2) % length) / length
    twiddle = np.zeros((2, padded, fast))
    twiddle[0, :kept] = np.cos(angle2)
    twiddle[1, :kept] = -np.sin(angle2)
    angle3 = 2.0 * np.pi * (np.outer(n2, n2) % fast) / fast
    cosine, sine = np.cos(angle3), np.sin(angle3)
    ahead = np.block([[cosine, -sine], [sine, cosine]])
    back = np.block([[cosine, sine], [-sine, cosine]])
    weight = np.where((k1 == 0) | (k1 == slow), 1.0, 2.0)[:, None] * (factor / length)
    last = np.zeros((slow, 2 * padded))
    last[:, :kept] = (weight * np.cos(angle1)).T
    last[:, padded : padded + kept] = (-weight * np.sin(angle1)).T
    return padded, first, twiddle, ahead, back, last


def joined(fast, group):
    return 2 if fast % 128 == 0 and group % 2 == 0 else 1


def core_kernel(n_chan, n_seq, padded, n_const, *refs):
    q_hbm, k_hbm, v_hbm, g_hbm, w_hbm, gain_hbm = refs[:6]
    const_hbm = refs[6 : 6 + n_const]
    out_pair, out_grad, out_gain = refs[6 + n_const : 9 + n_const]
    (
        q_ref, k_ref, v_ref, g_ref, in_tap, send_pair, in_pair, res_pair, send_lone, in_lone, res_lone, out_lone,
        lines, short, turned, spec, out_tap, hold,
    ) = refs[9 + n_const : 27 + n_const]
    consts = refs[27 + n_const : 27 + 2 * n_const]
    (
        load_sem, const_sem, own_sem, s_send, s_recv, t_send, t_recv, r_send, r_recv, b_send, b_recv,
        chan_ready,
    ) = refs[27 + 2 * n_const :]
    first_ref, twid_ref, ahead_ref, back_ref, last_ref = consts
    chan, seq = lax.axis_index("chan"), lax.axis_index("seq")
    _, pieces, group, fast = send_lone.shape
    slow = n_seq * pieces
    width = n_seq * group

    def each(count, act):
        def step(d, carry):
            act(d)
            return carry

        lax.fori_loop(1, count, step, 0)

    barrier = pltpu.get_barrier_semaphore()

    def greet(device):
        pl.semaphore_signal(barrier, inc=1, device_id=device, device_id_type=MESH)

    def tell(ready, device):
        pl.semaphore_signal(ready, inc=1, device_id=device, device_id_type=MESH)

    def span(low, high, act):
        def step(i, carry):
            act(i)
            return carry

        lax.fori_loop(low, high, step, 0)

    def pairwise(act):
        if n_seq & (n_seq - 1):
            others(act, seq, n_seq)
            return
        half = n_seq // 2
        for far in range(n_seq - 1, half - 1, -1):
            act(jnp.bitwise_xor(seq, far))
            if far > half:
                act(jnp.bitwise_xor(seq, far - half))

    def others(act, own, count):
        each(count, lambda d: act(lax.rem(own + d, count)))

    loads = [
        pltpu.make_async_copy(source, target, load_sem.at[i])
        for i, (source, target) in enumerate(
            [(k_hbm, k_ref), (v_hbm, v_ref), (g_hbm, g_ref), (q_hbm, q_ref), (gain_hbm, out_gain)]
        )
    ]
    others(lambda i: greet((chan, i)), seq, n_seq)
    for copy in loads[:2]:
        copy.start()
    span(chan + 1, n_chan, lambda i: greet((i, seq)))
    for copy in loads[2:]:
        copy.start()
    const_loads = [
        pltpu.make_async_copy(source, target, const_sem.at[i])
        for i, (source, target) in enumerate(zip(const_hbm, consts))
    ]

    def remote(source, target, send, recv, device):
        return pltpu.make_async_remote_copy(
            src_ref=source, dst_ref=target, send_sem=send, recv_sem=recv,
            device_id=device, device_id_type=MESH,
        )

    def at_slot(pair, lone, slot, peer, u):
        return lone.at[peer, u] if slot == 2 else pair.at[peer, slot, u]

    def sig_copy(kind, there, landing):
        source, target = ((send_pair, in_pair), (send_lone, in_lone))[kind]
        return remote(
            source.at[there], target.at[landing],
            s_send.at[kind, there], s_recv.at[kind, landing], (chan, there),
        )

    def res_copy(kind, there, landing):
        source, target = ((res_pair, out_pair), (res_lone, out_lone))[kind]
        return remote(
            source.at[there], target.at[landing],
            r_send.at[kind, there], r_recv.at[kind, landing], (chan, there),
        )

    def taps_of(at):
        return w_hbm.at[:, pl.ds(pl.multiple_of(at * width, width), width)]

    def tap_copy(there, landing):
        return remote(
            taps_of(there), in_tap.at[landing], t_send.at[there], t_recv.at[landing], (there, seq)
        )

    def back_copy(there, landing):
        return remote(
            out_lone.at[:, there], out_tap.at[landing], b_send.at[there], b_recv.at[landing],
            (there, seq),
        )

    def own_copy(source, target, index):
        return pltpu.make_async_copy(source, target, own_sem.at[index])

    own_sig = [
        own_copy(send_pair.at[seq], in_pair.at[seq], 0), own_copy(send_lone.at[seq], in_lone.at[seq], 1)
    ]
    own_res = [
        own_copy(res_pair.at[seq], out_pair.at[seq], 2), own_copy(res_lone.at[seq], out_lone.at[seq], 3)
    ]
    own_taps = own_copy(taps_of(chan), in_tap.at[chan], 4)
    own_back = own_copy(out_lone.at[:, chan], out_tap.at[chan], 5)
    own_taps.start()

    def pack(slot, pick):
        for u in range(pieces):
            flipped = pick(u).T
            for t in range(n_seq):
                at_slot(send_pair, send_lone, slot, t, u)[...] = flipped[t * group : (t + 1) * group].astype(BF16)

    def product(a_ref, b_ref):
        def pick(u):
            rows = pl.ds(u * fast, fast)
            return a_ref[rows, :].astype(F32) * b_ref[rows, :].astype(F32)

        return pick

    def send_tap(i):
        pl.semaphore_wait(chan_ready.at[i], 1)
        tap_copy(i, chan).start()

    loads[0].wait()
    loads[1].wait()
    pack(X, product(k_ref, v_ref))
    loads[2].wait()
    loads[3].wait()
    pack(G, product(g_ref, q_ref))
    pl.semaphore_wait(barrier, n_seq - 1 + chan)
    span(0, chan, lambda i: tell(chan_ready.at[chan], (i, seq)))
    own_sig[PAIR].start()
    pairwise(lambda i: sig_copy(PAIR, i, seq).start())
    span(0, chan, lambda i: tap_copy(i, chan).start())
    span(chan + 1, n_chan, send_tap)
    for copy in const_loads:
        copy.start()
    own_taps.wait()
    others(lambda i: tap_copy(i, i).wait(), chan, n_chan)
    pack(F, lambda u: in_tap[u].astype(F32))
    own_sig[LONE].start()
    pairwise(lambda i: sig_copy(LONE, i, seq).start())
    for copy in const_loads:
        copy.wait()

    cosine, sine = twid_ref[0], twid_ref[1]
    batch = joined(fast, group)

    def times(table, columns):
        if batch == 1:
            return [dot(table, column) for column in columns]
        wide = dot(table, jnp.concatenate(columns, axis=1))
        return [wide[:, i * fast : (i + 1) * fast] for i in range(len(columns))]

    def through(target, slot, table, fine):
        x = short[slot]
        if fine:
            target[slot] = dot(jnp.concatenate([x, x], axis=1), table[...])
        else:
            target[slot] = dot(x, table[: 2 * fast, :])

    def forward(slots):
        for s in range(n_seq):
            for u in range(pieces):
                at = pl.ds((s * pieces + u) * group, group)
                for slot in slots:
                    lines[slot, at, :] = at_slot(in_pair, in_lone, slot, s, u)[...].astype(F32)
        for base in range(0, group, batch):
            for slot in slots:
                columns = []
                for c in range(base, base + batch):
                    column = lines[slot, pl.ds(c, slow, stride=group), :].astype(BF16)
                    columns.append(jnp.concatenate([column, column], axis=0))
                rows = []
                for got in times(first_ref[...], columns):
                    real, imag = got[:padded], got[padded:]
                    rows.append(
                        jnp.concatenate([real * cosine - imag * sine, real * sine + imag * cosine], axis=1)
                    )
                at = pl.ds(base * padded, batch * padded)
                short[slot, at, :] = jnp.concatenate(rows, axis=0).astype(BF16)
        for slot in slots:
            through(turned, slot, ahead_ref, slot != F)

    def inverse(jobs):
        for base in range(0, group, batch):
            at = pl.ds(base * padded, batch * padded)
            for slot, a, b, conjugate in jobs:
                ar, ai = turned[a, at, :fast], turned[a, at, fast:]
                br, bi = turned[b, at, :fast], turned[b, at, fast:]
                if conjugate:
                    real, imag = ar * br + ai * bi, ar * bi - ai * br
                else:
                    real, imag = ar * br - ai * bi, ar * bi + ai * br
                short[slot, at, :] = jnp.concatenate([real, imag], axis=1).astype(BF16)
        for slot, *_ in jobs:
            through(spec, slot, back_ref, slot == GRAD)
        for base in range(0, group, batch):
            for slot, *_ in jobs:
                columns = []
                for c in range(base, base + batch):
                    at = pl.ds(c * padded, padded)
                    real, imag = spec[slot, at, :fast], spec[slot, at, fast:]
                    real, imag = real * cosine + imag * sine, imag * cosine - real * sine
                    both = jnp.concatenate([real, imag], axis=0).astype(BF16)
                    columns.append(jnp.concatenate([both, both], axis=0))
                for c, got in zip(range(base, base + batch), times(last_ref[...], columns)):
                    lines[slot, pl.ds(c, slow, stride=group), :] = got
        for s in range(n_seq):
            for u in range(pieces):
                at = pl.ds((s * pieces + u) * group, group)
                for slot, *_ in jobs:
                    at_slot(res_pair, res_lone, slot, s, u)[...] = lines[slot, at, :].astype(BF16)

    def landed(kind):
        own_sig[kind].wait()
        others(lambda i: sig_copy(kind, i, i).wait(), seq, n_seq)

    def reply(kind):
        own_res[kind].start()
        others(lambda i: res_copy(kind, i, seq).start(), seq, n_seq)

    def arrive(kind):
        own_res[kind].wait()
        others(lambda i: res_copy(kind, i, i).wait(), seq, n_seq)

    landed(PAIR)
    forward((X, G))
    inverse(((GRAD, X, G, True),))
    reply(LONE)
    landed(LONE)
    forward((F,))
    inverse(((Y, F, X, False), (BACK, F, G, True)))
    reply(PAIR)
    arrive(LONE)
    others(lambda i: back_copy(i, chan).start(), chan, n_chan)
    own_back.start()
    own_back.wait()
    others(lambda i: back_copy(i, i).wait(), chan, n_chan)
    for a in range(pieces):
        for t in range(n_seq):
            hold[a, pl.ds(t * group, group), :] = out_tap[a, t].astype(F32)
        out_grad[pl.ds(a, fast, stride=pieces), :] = hold[a].T
    loads[4].wait()
    arrive(PAIR)


def after_kernel(
    q_ref, k_ref, v_ref, g_ref, gain_ref, sig_ref, grad_ref, m_hbm, qg_hbm, kg_hbm, vg_hbm, fg_hbm,
    m_ref, qg_ref, kg_ref, vg_ref, hold, sem,
):
    seq_parts, _, pieces, group, fast = sig_ref.shape
    gain = gain_ref[...]
    copies = []

    def write(source, target):
        copies.append(pltpu.make_async_copy(source, target, sem.at[len(copies)]))
        copies[-1].start()

    def columns(slot, u):
        for t in range(seq_parts):
            hold[slot, u, pl.ds(t * group, group), :] = sig_ref[t, slot, u].astype(F32)
        return hold[slot, u].T

    write(grad_ref, fg_hbm)
    for u in range(pieces):
        rows = pl.ds(u * fast, fast)
        query, key = q_ref[rows, :].astype(F32), k_ref[rows, :].astype(F32)
        value, grad = v_ref[rows, :].astype(F32), g_ref[rows, :].astype(F32)
        state = columns(Y, u) + gain * (key * value)
        m_ref[rows, :] = (query * state).astype(BF16)
        qg_ref[rows, :] = (grad * state).astype(BF16)
        back = columns(BACK, u) + gain * (grad * query)
        kg_ref[rows, :] = (back * value).astype(BF16)
        vg_ref[rows, :] = (back * key).astype(BF16)
        for source, target in ((m_ref, m_hbm), (qg_ref, qg_hbm), (kg_ref, kg_hbm), (vg_ref, vg_hbm)):
            write(source.at[rows, :], target.at[rows, :])
    for copy in copies:
        copy.wait()


def body(n_chan, n_seq, query, key, value, filter_weights, skip_gain, cotangent):
    rows, width = query.shape
    tap_rows, _, all_width = filter_weights.shape
    fast, group, pieces = tap_rows, width // n_seq, n_chan
    slow = rows * n_seq // fast
    padded, first, twiddle, ahead, back, last = tables(
        slow, fast, 1.0 / math.sqrt(rows * n_seq), 16 // joined(fast, group)
    )
    weights = filter_weights.reshape(tap_rows, all_width)
    consts = [
        jnp.concatenate(split_table(first), axis=1),
        jnp.asarray(twiddle, F32),
        jnp.concatenate(split_table(ahead), axis=0),
        jnp.concatenate(split_table(back), axis=0),
        jnp.concatenate(split_table(last), axis=1),
    ]
    pair_dims = (n_seq, 2, pieces, group, fast)
    lone_dims = (n_seq, pieces, group, fast)
    tap_dims = (n_chan, n_seq, group, fast)
    flat_dims = (rows, width)
    dma = pltpu.SemaphoreType.DMA
    anywhere = pl.BlockSpec(memory_space=pl.ANY)
    vmem = pl.BlockSpec(memory_space=pltpu.VMEM)
    sig, taps, gain = pl.pallas_call(
        functools.partial(core_kernel, n_chan, n_seq, padded, len(consts)),
        out_shape=[pltpu.VMEM(pair_dims, BF16), pltpu.VMEM((tap_rows * n_chan, width), F32), pltpu.VMEM((1, width), F32)],
        in_specs=[anywhere] * (6 + len(consts)),
        out_specs=[vmem] * 3,
        scratch_shapes=[
            *[pltpu.VMEM(flat_dims, BF16)] * 4,
            pltpu.VMEM((n_chan, tap_rows, width), BF16),
            *[pltpu.VMEM(pair_dims, BF16)] * 3,
            *[pltpu.VMEM(lone_dims, BF16)] * 4,
            pltpu.VMEM((3, slow * group, fast), F32),
            pltpu.VMEM((3, group * padded, 2 * fast), BF16),
            pltpu.VMEM((3, group * padded, 2 * fast), F32),
            pltpu.VMEM((3, group * padded, 2 * fast), F32),
            pltpu.VMEM(tap_dims, BF16),
            pltpu.VMEM((n_chan, width, fast), F32),
            *[pltpu.VMEM(const.shape, const.dtype) for const in consts],
            dma((5,)),
            dma((len(consts),)),
            dma((6,)),
            dma((2, n_seq)),
            dma((2, n_seq)),
            dma((n_chan,)),
            dma((n_chan,)),
            dma((2, n_seq)),
            dma((2, n_seq)),
            dma((n_chan,)),
            dma((n_chan,)),
            pltpu.SemaphoreType.REGULAR((n_chan,)),
        ],
        compiler_params=pltpu.CompilerParams(
            collective_id=0, has_side_effects=True, vmem_limit_bytes=60 * 1024 * 1024
        ),
        name="core",
    )(query, key, value, cotangent, weights, skip_gain.reshape(1, width), *consts)
    flat = jax.ShapeDtypeStruct(flat_dims, BF16)
    outs = pl.pallas_call(
        after_kernel,
        out_shape=[flat, flat, flat, flat, jax.ShapeDtypeStruct((tap_rows * n_chan, width), F32)],
        in_specs=[vmem] * 7,
        out_specs=[anywhere] * 5,
        scratch_shapes=[
            *[pltpu.VMEM(flat_dims, BF16)] * 4,
            pltpu.VMEM((2, pieces, width, fast), F32),
            dma((1 + 4 * pieces,)),
        ],
        compiler_params=pltpu.CompilerParams(vmem_limit_bytes=24 * 1024 * 1024),
        name="after",
    )(query, key, value, cotangent, gain, sig, taps)
    return (*outs[:4], outs[4].reshape(tap_rows, 1, all_width))


def solution(mesh):
    n_chan, n_seq = mesh.shape["chan"], mesh.shape["seq"]
    block = P("seq", "chan")
    taps = P("chan", "seq", None)
    return jax.shard_map(
        functools.partial(body, n_chan, n_seq),
        mesh=mesh,
        in_specs=(block, block, block, taps, P("chan"), block),
        out_specs=(block, block, block, block, taps),
        check_vma=False,
    )
```
